512 devices in a mesh: ctx: 128 (over y, z_hi, x, core), ch: 4 (over z_lo).
Axes of the slice: x: 4, y: 8, z: 8 (z_hi: 2, z_lo: 4; z = z_hi * 4 + z_lo), core: 2. Of those that a mesh axis runs over, the one named last changes fastest.
Arguments:
- queries: bfloat16 [16384, 8192], P('ctx', 'ch'), may hold values from -6 to 6
- key_input: bfloat16 [16384, 8192], P('ctx', 'ch'), may hold values from -6 to 6
- value_input: bfloat16 [16384, 8192], P('ctx', 'ch'), may hold values from -6 to 6
- cotangent: bfloat16 [16384, 8192], P('ctx', 'ch'), may hold values from -60 to 60, as said below
- residues: float32 [512, 16], replicated, may hold values from -1 to 1
- log_rates: float32 [512, 16], replicated, may hold values from -14 to -3
- skip_gain: float32 [8192], replicated, may hold values from -1 to 1
Outputs:
- grad_query: bfloat16 [16384, 8192], P('ctx', 'ch')
- grad_key: bfloat16 [16384, 8192], P('ctx', 'ch')
- grad_value: bfloat16 [16384, 8192], P('ctx', 'ch')
- grad_residue: float32 [512, 16], replicated
- grad_lograte: float32 [512, 16], replicated
- grad_skip: float32 [8192], replicated
The draws below stay inside these ranges and needn't reach their ends.
Inputs may be any that keep to these rules, and one draw needn't show every extreme that they name: Every row of the cotangent has its own scale.
All inputs are finite; a program needn't handle non-finite values.
Results may differ from the reference program's by a relative error of at most 0.017.
Values may be sent and summed in bfloat16 or wider, within the bound.
A program may use at most 64 MiB of HBM per device.

```python
import math
import jax
import jax.numpy as jnp
from jax import lax

D = 8192
GROUP = 16
POLES = 16
TOKENS = 16384
GROUPS = 512


def pole_logs(key):
    base = jax.random.fold_in(key, 7)
    pick_key, slow_key, middle_key, fast_key = jax.random.split(base, 4)
    length = float(TOKENS)
    shape = (GROUPS, POLES)
    slow_share = 0.5
    middle_cut = 0.75
    fast_low = math.log(1.0 / 50.0)
    fast_high = math.log(1.0 / 30.0)
    slow_low = math.log(0.2 / length)
    slow_high = min(math.log(2.0 / length), fast_high)
    middle_low = min(math.log(2.0 / length), fast_low)
    choose = jax.random.uniform(pick_key, shape)
    slow = jax.random.uniform(slow_key, shape, minval=slow_low, maxval=slow_high)
    middle = jax.random.uniform(middle_key, shape, minval=middle_low, maxval=fast_low)
    fast = jax.random.uniform(fast_key, shape, minval=fast_low, maxval=fast_high)
    return jnp.where(choose < slow_share, slow, jnp.where(choose < middle_cut, middle, fast))


def draw_log_rates(key, part):
    return pole_logs(key).astype(jnp.float32)


def draw_residues(key, part):
    decay_rate = jnp.exp(pole_logs(key))
    noise_key = jax.random.fold_in(key, 8)
    shape = (GROUPS, POLES)
    noise = jnp.clip(jax.random.normal(noise_key, shape), -4.0, 4.0)
    return (noise * 0.3 * jnp.sqrt(2.0 * decay_rate)).astype(jnp.float32)


def draw_cotangent(key, part):
    noise_key = jax.random.fold_in(jax.random.fold_in(key, 9), 0)
    shape = (TOKENS, D)
    fraction = jnp.arange(TOKENS).astype(jnp.float32) / float(TOKENS)
    noise = jnp.clip(jax.random.normal(noise_key, shape), -5.0, 5.0)
    row_scale = 1.0 + 2.0 * fraction
    return (noise * row_scale[:, None]).astype(jnp.bfloat16)


def shard_levels(rng, dims, cuts, smallest, largest):
    gain = 1.0
    for position, blocks in cuts:
        steps = jax.random.uniform(jax.random.fold_in(jax.random.fold_in(rng, 6), position), (blocks,), jnp.float32, smallest / len(cuts), largest / len(cuts))
        gain = gain * jnp.repeat(jnp.exp(steps), dims[position] // blocks).reshape((-1,) + (1,) * (len(dims) - 1 - position))
    return gain


def centred(own_key, dims, deviation, most, shards=(), kind=jnp.bfloat16):
    result = jax.random.normal(own_key, dims, jnp.float32) * deviation
    if len(shards) > 0:
        result = shard_levels(own_key, dims, shards, -0.22, 0.18) * result
    return jnp.clip(result, min=-most, max=most).astype(kind)


def setup_inputs(seed: int = 0) -> dict:
    key_of = jax.random.split(jax.random.key(seed), 8)
    return {
        "queries": centred(key_of[0], (TOKENS, D), 1.0, 6.0, ((0, 128), (1, 4))),
        "key_input": centred(key_of[1], (TOKENS, D), 1.0, 6.0, ((0, 128), (1, 4))),
        "value_input": centred(key_of[2], (TOKENS, D), 1.0, 6.0, ((0, 128), (1, 4))),
        "cotangent": draw_cotangent(jax.random.fold_in(key_of[7], 71), 0),
        "residues": draw_residues(jax.random.fold_in(key_of[7], 71), 0),
        "log_rates": draw_log_rates(jax.random.fold_in(key_of[7], 71), 0),
        "skip_gain": jnp.clip(jax.random.uniform(key_of[6], (D,), jnp.float32, -1.0, 1.0), -1.0, 1.0),
    }


def reference(queries, key_input, value_input, cotangent, residues, log_rates, skip_gain):
    length = TOKENS
    padded = 2 * length
    groups = D // GROUP
    gated = (key_input.astype(jnp.float32) * value_input.astype(jnp.float32)).astype(jnp.bfloat16)
    dgate = (cotangent.astype(jnp.float32) * queries.astype(jnp.float32)).astype(jnp.bfloat16)
    decay_rate = jnp.exp(log_rates)
    positions = jnp.arange(length).astype(jnp.float32)
    gated_groups = gated.astype(jnp.float32).reshape(length, groups, GROUP).transpose(1, 2, 0)
    dgate_groups = dgate.astype(jnp.float32).reshape(length, groups, GROUP).transpose(1, 2, 0)

    def one_group(member):
        gated_one, dgate_one, residue_one, rate_one = member
        decays = jnp.exp(-rate_one[:, None] * positions[None, :])
        filter_taps = lax.optimization_barrier(jnp.sum(residue_one[:, None] * decays, axis=0))
        filter_spec = jnp.fft.rfft(filter_taps, n=padded)
        gated_spec = jnp.fft.rfft(gated_one, n=padded, axis=1)
        dgate_spec = jnp.fft.rfft(dgate_one, n=padded, axis=1)
        conv_z = jnp.fft.irfft(filter_spec[None, :] * gated_spec, n=padded, axis=1)[:, :length]
        conv_flow = jnp.fft.irfft(jnp.conj(filter_spec)[None, :] * dgate_spec, n=padded, axis=1)[:, :length]
        cross_spec = lax.optimization_barrier(jnp.sum(jnp.conj(gated_spec) * dgate_spec, axis=0))
        filter_grad = jnp.fft.irfft(cross_spec, n=padded)[:length].astype(jnp.float32)
        grad_res = jnp.dot(decays, filter_grad, precision=lax.Precision.HIGHEST)
        grad_log = -rate_one * residue_one * jnp.dot(decays * positions[None, :], filter_grad, precision=lax.Precision.HIGHEST)
        return (conv_z.astype(jnp.float32), conv_flow.astype(jnp.float32), grad_res, grad_log)
    conv_z, conv_flow, grad_res, grad_log = lax.map(one_group, (gated_groups, dgate_groups, residues, decay_rate))
    conv_z = conv_z.transpose(2, 0, 1).reshape(length, D)
    conv_flow = conv_flow.transpose(2, 0, 1).reshape(length, D)
    hidden_z = (skip_gain[None, :] * gated.astype(jnp.float32) + conv_z).astype(jnp.bfloat16)
    flow = (skip_gain[None, :] * dgate.astype(jnp.float32) + conv_flow).astype(jnp.bfloat16)
    grad_query = (cotangent.astype(jnp.float32) * hidden_z.astype(jnp.float32)).astype(jnp.bfloat16)
    grad_key = (flow.astype(jnp.float32) * value_input.astype(jnp.float32)).astype(jnp.bfloat16)
    grad_value = (flow.astype(jnp.float32) * key_input.astype(jnp.float32)).astype(jnp.bfloat16)
    grad_skip = lax.optimization_barrier(jnp.sum(dgate.astype(jnp.float32) * gated.astype(jnp.float32), axis=0)) / math.sqrt(length)
    return (grad_query, grad_key, grad_value, grad_res / length, grad_log / math.sqrt(length), grad_skip)
```

```python
import functools
import math

import jax
import jax.numpy as jnp
from jax import lax
from jax.experimental import pallas as pl
from jax.experimental.pallas import tpu as pltpu
from jax.sharding import PartitionSpec as P

GROUP = 16
POLES = 16
OWN = 8
BLK = 256
TOK = 128

MESH = pl.DeviceIdType.MESH
F32 = jnp.float32
BF16 = jnp.bfloat16
HIGHEST = lax.Precision.HIGHEST


def iota(shape, dim):
    return lax.broadcasted_iota(jnp.int32, shape, dim)


def dot(a, b, dims=((1,), (0,)), precision=None):
    return lax.dot_general(
        a, b, (dims, ((), ())), precision=precision, preferred_element_type=F32
    )


def comm_kernel(
    nsb, nch,
    q_ref, k_ref, v_ref, c_ref, res_ref, log_ref, skip_ref,
    z_ref, f_ref, g_ref,
    x_s, d_s, ed_s, el_s, ed2_s, el2_s, h_s, hr_s, zl_s, fl_s,
    p1s, p1r, p2s, p2r, p3s, p3r, pbs, pbr, p4s, p4r, p5s, p5r,
    s1, r1, s2, r2, s3, r3, sb_, rb_, s4, r4, s5, r5,
):
    ctx = lax.axis_index("ctx")
    ch = lax.axis_index("ch")
    own = ctx % OWN
    sup = ctx // OWN

    barrier = pltpu.get_barrier_semaphore()

    def greet(ctx_to, ch_to):
        pl.semaphore_signal(barrier, inc=1, device_id=(ctx_to, ch_to), device_id_type=MESH)

    @pl.loop(1, OWN)
    def _(j):
        greet(sup * OWN + (own + j) % OWN, ch)

    @pl.loop(1, nsb)
    def _(j):
        greet(((sup + j) % nsb) * OWN + own, ch)

    @pl.loop(1, nch)
    def _(i):
        @pl.loop(0, OWN)
        def _(j):
            greet(sup * OWN + j, (ch + i) % nch)

    lane_t = iota((GROUP, TOK), 1).astype(F32)
    same_group = (iota((BLK, BLK), 0) % 16) == (iota((BLK, BLK), 1) // 16)
    pick_pole = ((iota((POLES, BLK), 1) // 16) == iota((POLES, BLK), 0)).astype(BF16)
    spread_pole = ((iota((BLK, POLES), 0) // 16) == iota((BLK, POLES), 1)).astype(BF16)

    @pl.loop(0, OWN)
    def _(i):
        rows = pl.ds(pl.multiple_of(ch * 128 + i * 16, 16), 16)
        cols = pl.ds(pl.multiple_of(i * BLK, BLK), BLK)
        lam = jnp.exp(log_ref[rows, :])
        res = res_ref[rows, :]
        taps = jnp.zeros((GROUP, TOK), F32)
        back = jnp.zeros((GROUP, TOK), F32)
        for p in range(POLES):
            lam_p = lam[:, p : p + 1]
            res_p = res[:, p : p + 1]
            ed = jnp.exp(-lam_p * lane_t)
            el = jnp.exp(-lam_p * (TOK - 1.0 - lane_t))
            at = pl.ds(p * 16, 16)
            ed_s[i, at, :] = ed.astype(BF16)
            el_s[i, at, :] = el.astype(BF16)
            ed2_s[i, at, :] = (ed * (lane_t + 1.0)).astype(BF16)
            el2_s[i, at, :] = (el * (TOK - 1.0 - lane_t)).astype(BF16)
            taps = taps + res_p * ed
            back = back + (res_p * jnp.exp(-lam_p)) * el
        h_s[i] = taps
        hr_s[i] = jnp.where(lane_t == 0.0, taps, back)
        x = (k_ref[:, cols].astype(F32) * v_ref[:, cols].astype(F32)).astype(BF16)
        d = (c_ref[:, cols].astype(F32) * q_ref[:, cols].astype(F32)).astype(BF16)
        x_s[:, cols] = x
        d_s[:, cols] = d
        pbs[i, 2:3, :] = jnp.sum(x.astype(F32) * d.astype(F32), axis=0, keepdims=True)
        for n, (table, val) in enumerate(((el_s, x), (ed_s, d), (el2_s, x), (ed2_s, d))):
            full = dot(table[i], val)
            full = jnp.where(same_group, full, 0.0).astype(BF16)
            p1s[i, n] = dot(pick_pole, full).astype(BF16)

    pl.semaphore_wait(barrier, (OWN - 1) + (nsb - 1) + (nch - 1) * OWN)

    def to_own(j, src, dst, send, recv):
        other = (own + j) % OWN
        return pltpu.make_async_remote_copy(
            src_ref=src.at[other], dst_ref=dst.at[own], send_sem=send.at[other], recv_sem=recv.at[own],
            device_id=(sup * OWN + other, ch), device_id_type=MESH,
        )

    def from_own(j, src, dst, send, recv):
        other = (own + j) % OWN
        return pltpu.make_async_remote_copy(
            src_ref=src.at[other], dst_ref=dst.at[other], send_sem=send.at[other], recv_sem=recv.at[other],
            device_id=(sup * OWN + other, ch), device_id_type=MESH,
        )

    def send_own(*args):
        @pl.loop(1, OWN)
        def _(j):
            to_own(j, *args).start()

    def wait_own(*args):
        @pl.loop(1, OWN)
        def _(j):
            from_own(j, *args).wait_recv()

    def sent_own(*args):
        @pl.loop(1, OWN)
        def _(j):
            from_own(j, *args).wait_send()

    send_own(p1s, p1r, s1, r1)
    p1r[own] = p1s[own]
    p2r[sup] = jnp.zeros((POLES, BLK), BF16)

    row_t = iota((TOK, TOK), 0)
    col_t = iota((TOK, TOK), 1)
    lane_group = iota((TOK, BLK), 1) // 16

    @pl.loop(0, OWN)
    def _(i):
        cols = pl.ds(pl.multiple_of(i * BLK, BLK), BLK)
        x = x_s[:, cols]
        acc = jnp.zeros((TOK, BLK), F32)
        hr = hr_s[i]
        for g in range(16):
            wide = jnp.broadcast_to(hr[g : g + 1, :], (TOK, TOK))
            mat = pltpu.roll(wide, 0, 1, stride=1, stride_axis=0)
            mat = jnp.where(col_t <= row_t, mat, 0.0).astype(BF16)
            acc = jnp.where(lane_group == g, dot(mat, x), acc)
        zl_s[:, cols] = acc

    rows = pl.ds(pl.multiple_of(ch * 128 + own * 16, 16), 16)
    lam_own = jnp.exp(log_ref[rows, :])
    res_own = res_ref[rows, :]
    to_chan = ((iota((16, BLK), 1) // 16) == iota((16, BLK), 0)).astype(F32)
    lam_pc = dot(lam_own, to_chan, ((0,), (0,)), HIGHEST)
    res_pc = dot(res_own, to_chan, ((0,), (0,)), HIGHEST)
    w = jnp.exp(-float(TOK) * lam_pc)
    e1 = jnp.exp(-lam_pc)
    re1 = res_pc * e1

    wait_own(p1s, p1r, s1, r1)
    sum_l = jnp.zeros((POLES, BLK), F32)
    sum_d = jnp.zeros((POLES, BLK), F32)
    for b in range(OWN):
        sum_l = w * sum_l + p1r[b, 0].astype(F32)
        sum_d = w * sum_d + p1r[OWN - 1 - b, 1].astype(F32)
    p2s[0] = sum_l.astype(BF16)
    p2s[1] = sum_d.astype(BF16)

    def sup_copy(j, slot):
        other = (sup + j) % nsb
        later = (other > sup).astype(jnp.int32)
        return pltpu.make_async_remote_copy(
            src_ref=p2s.at[1 - later], dst_ref=p2r.at[slot], send_sem=s2.at[other], recv_sem=r2.at[slot],
            device_id=(other * OWN + own, ch), device_id_type=MESH,
        )

    @pl.loop(1, nsb)
    def _(j):
        sup_copy(j, sup).start()

    lane_row = iota((16, BLK), 1)
    diag = (lane_row % 16) == iota((16, BLK), 0)
    flip = (row_t == TOK - 1 - col_t).astype(BF16)

    @pl.loop(0, OWN)
    def _(i):
        cols = pl.ds(pl.multiple_of(i * BLK, BLK), BLK)
        x = dot(flip, x_s[:, cols]).astype(BF16)
        d = d_s[:, cols]
        sums = []
        for g in range(16):
            dm = jnp.where(lane_group == g, d, jnp.zeros_like(d))
            corr = dot(x, dm, ((1,), (1,)))
            corr = jnp.where(col_t >= TOK - 1 - row_t, corr, 0.0)
            corr = pltpu.roll(corr, 1, 1, stride=1, stride_axis=0)
            sums.append(jnp.sum(corr, axis=0, keepdims=True))
        fg = jnp.concatenate(sums, axis=0)
        hi = fg.astype(BF16)
        lo = (fg - hi.astype(F32)).astype(BF16)
        both = jnp.concatenate([hi, lo], axis=0)
        r_in = dot(both, ed_s[i], ((1,), (1,)))
        m_in = dot(both, ed2_s[i], ((1,), (1,)))
        r_in = r_in[:16] + r_in[16:]
        m_in = m_in[:16] + m_in[16:] - r_in
        pbs[i, 0:1, :] = jnp.sum(jnp.where(diag, r_in, 0.0), axis=0, keepdims=True)
        pbs[i, 1:2, :] = jnp.sum(jnp.where(diag, m_in, 0.0), axis=0, keepdims=True)
        pbs[i, 3:4, :] = jnp.zeros((1, BLK), F32)

    send_own(pbs, pbr, sb_, rb_)
    pbr[own] = pbs[own]

    @pl.loop(0, OWN)
    def _(i):
        cols = pl.ds(pl.multiple_of(i * BLK, BLK), BLK)
        d = d_s[:, cols]
        acc = jnp.zeros((TOK, BLK), F32)
        h = h_s[i]
        for g in range(16):
            wide = jnp.broadcast_to(h[g : g + 1, :], (TOK, TOK))
            mat = pltpu.roll(wide, 0, 1, stride=1, stride_axis=0)
            mat = jnp.where(col_t >= row_t, mat, 0.0).astype(BF16)
            acc = jnp.where(lane_group == g, dot(mat, d), acc)
        fl_s[:, cols] = acc

    @pl.loop(1, nsb)
    def _(j):
        sup_copy(j, (sup + j) % nsb).wait_recv()

    in_s = jnp.zeros((POLES, BLK), F32)
    in_f = jnp.zeros((POLES, BLK), F32)
    for b in range(nsb):
        gap = jnp.maximum(jnp.abs(sup - b) - 1, 0).astype(F32) * float(TOK * OWN)
        term = jnp.exp(-lam_pc * gap) * p2r[b].astype(F32)
        in_s = in_s + jnp.where(b < sup, term, 0.0)
        in_f = in_f + jnp.where(b > sup, term, 0.0)
    carry_s = []
    for b in range(OWN):
        carry_s.append(in_s)
        p3s[b, 0] = (re1 * in_s).astype(BF16)
        in_s = w * in_s + p1r[b, 0].astype(F32)
    r_sum = jnp.zeros((POLES, BLK), F32)
    m_sum = jnp.zeros((POLES, BLK), F32)
    for b in reversed(range(OWN)):
        p3s[b, 1] = (re1 * in_f).astype(BF16)
        d_b = p1r[b, 1].astype(F32)
        r_sum = r_sum + d_b * carry_s[b]
        m_sum = (
            m_sum
            + p1r[b, 3].astype(F32) * carry_s[b]
            + p1r[b, 2].astype(F32) * in_f
            + (float(TOK) * w) * (carry_s[b] * in_f)
        )
        in_f = w * in_f + d_b
    send_own(p3s, p3r, s3, r3)
    p3r[own] = p3s[own]

    chan_group = ((iota((BLK, BLK), 0) // 16) == (iota((BLK, BLK), 1) % 16)).astype(F32)
    pole_row = (iota((POLES, BLK), 1) // 16) == iota((POLES, BLK), 0)
    sums = dot(jnp.concatenate([r_sum * e1, m_sum * e1], axis=0), chan_group, precision=HIGHEST)
    r_row = jnp.sum(jnp.where(pole_row, sums[:POLES], 0.0), axis=0, keepdims=True)
    m_row = jnp.sum(jnp.where(pole_row, sums[POLES:], 0.0), axis=0, keepdims=True)
    wait_own(pbs, pbr, sb_, rb_)
    part = pbr[0]
    for b in range(1, OWN):
        part = part + pbr[b]
    p4s[0:1, :] = part[0:1] + r_row
    p4s[1:2, :] = part[1:2] + m_row
    p4s[2:4, :] = part[2:4]

    def grad_copy(j, slot):
        other = (sup + j) % nsb
        return pltpu.make_async_remote_copy(
            src_ref=p4s, dst_ref=p4r.at[slot], send_sem=s4.at[other], recv_sem=r4.at[slot],
            device_id=(other * OWN + own, ch), device_id_type=MESH,
        )

    @pl.loop(1, nsb)
    def _(j):
        grad_copy(j, sup).start()

    p4r[sup] = p4s[...]

    wait_own(p3s, p3r, s3, r3)

    @pl.loop(0, OWN)
    def _(i):
        cols = pl.ds(pl.multiple_of(i * BLK, BLK), BLK)
        skip = skip_ref[:, pl.ds(pl.multiple_of(ch * (OWN * BLK) + i * BLK, BLK), BLK)]
        for n, (table, src, loc, out) in enumerate(
            ((ed_s, x_s, zl_s, z_ref), (el_s, d_s, fl_s, f_ref))
        ):
            wide = dot(spread_pole, p3r[i, n])
            wide = jnp.where(same_group, wide, 0.0).astype(BF16)
            corr = dot(table[i], wide, ((0,), (0,)))
            out[:, cols] = (skip * src[:, cols].astype(F32) + (loc[:, cols] + corr)).astype(BF16)

    to_pole = ((iota((POLES, BLK), 1) // 16) == iota((POLES, BLK), 0)).astype(F32)
    scale = dot(-lam_own * res_own, to_pole, precision=HIGHEST)
    scale_row = jnp.sum(jnp.where(diag, scale, 0.0), axis=0, keepdims=True)
    length = float(TOK * OWN * nsb)

    @pl.loop(1, nsb)
    def _(j):
        grad_copy(j, (sup + j) % nsb).wait_recv()

    total = p4r[0]
    for b in range(1, nsb):
        total = total + p4r[b]
    p5s[0:1, :] = total[0:1] / length
    p5s[1:2, :] = total[1:2] * scale_row / math.sqrt(length)
    p5s[2:4, :] = total[2:4] / math.sqrt(length)

    def last_copy(i, j, mine):
        ch_to = (ch + i) % nch
        own_to = (own + j) % OWN
        here = ch * OWN + own
        there = ch_to * OWN + own_to
        slot = here if mine else there
        return pltpu.make_async_remote_copy(
            src_ref=p5s, dst_ref=p5r.at[slot], send_sem=s5.at[there], recv_sem=r5.at[slot],
            device_id=(sup * OWN + own_to, ch_to), device_id_type=MESH,
        )

    @pl.loop(1, nch * OWN)
    def _(n):
        last_copy(n // OWN, n % OWN, True).start()

    p5r[ch * OWN + own] = p5s[...]

    sent_own(p1s, p1r, s1, r1)
    sent_own(pbs, pbr, sb_, rb_)
    sent_own(p3s, p3r, s3, r3)

    @pl.loop(1, nsb)
    def _(j):
        sup_copy(j, sup).wait_send()
        grad_copy(j, sup).wait_send()

    @pl.loop(1, nch * OWN)
    def _(n):
        last_copy(n // OWN, n % OWN, False).wait_recv()

    @pl.loop(1, nch * OWN)
    def _(n):
        last_copy(n // OWN, n % OWN, True).wait_send()

    g_ref[...] = p5r[...]


def exchange(queries, key_input, value_input, cotangent, residues, log_rates, skip_row):
    nsb = lax.axis_size("ctx") // OWN
    nch = lax.axis_size("ch")
    width = OWN * BLK
    vmem = pl.BlockSpec(memory_space=pltpu.VMEM)
    dma = pltpu.SemaphoreType.DMA
    state = (POLES, BLK)
    return pl.pallas_call(
        functools.partial(comm_kernel, nsb, nch),
        out_shape=(
            jax.ShapeDtypeStruct((TOK, width), BF16),
            jax.ShapeDtypeStruct((TOK, width), BF16),
            jax.ShapeDtypeStruct((nch * OWN, 4, BLK), F32),
        ),
        in_specs=[vmem] * 7,
        out_specs=(vmem, vmem, vmem),
        scratch_shapes=[
            pltpu.VMEM((TOK, width), BF16),
            pltpu.VMEM((TOK, width), BF16),
            *[pltpu.VMEM((OWN, BLK, TOK), BF16)] * 4,
            pltpu.VMEM((OWN, GROUP, TOK), F32),
            pltpu.VMEM((OWN, GROUP, TOK), F32),
            pltpu.VMEM((TOK, width), F32),
            pltpu.VMEM((TOK, width), F32),
            pltpu.VMEM((OWN, 4) + state, BF16),
            pltpu.VMEM((OWN, 4) + state, BF16),
            pltpu.VMEM((2,) + state, BF16),
            pltpu.VMEM((nsb,) + state, BF16),
            pltpu.VMEM((OWN, 2) + state, BF16),
            pltpu.VMEM((OWN, 2) + state, BF16),
            pltpu.VMEM((OWN, 4, BLK), F32),
            pltpu.VMEM((OWN, 4, BLK), F32),
            pltpu.VMEM((4, BLK), F32),
            pltpu.VMEM((nsb, 4, BLK), F32),
            pltpu.VMEM((4, BLK), F32),
            pltpu.VMEM((nch * OWN, 4, BLK), F32),
            dma((OWN,)), dma((OWN,)),
            dma((nsb,)), dma((nsb,)),
            dma((OWN,)), dma((OWN,)),
            dma((OWN,)), dma((OWN,)),
            dma((nsb,)), dma((nsb,)),
            dma((nch * OWN,)), dma((nch * OWN,)),
        ],
        compiler_params=pltpu.CompilerParams(
            collective_id=0, has_side_effects=True, vmem_limit_bytes=48 << 20
        ),
        name="exchange",
    )(queries, key_input, value_input, cotangent, residues, log_rates, skip_row)


def finish_kernel(z_ref, f_ref, c_ref, k_ref, v_ref, g_ref, gq_ref, gk_ref, gv_ref, gr_ref, gl_ref, gs_ref):
    gq_ref[...] = (c_ref[...].astype(F32) * z_ref[...].astype(F32)).astype(BF16)
    flow = f_ref[...].astype(F32)
    gk_ref[...] = (flow * v_ref[...].astype(F32)).astype(BF16)
    gv_ref[...] = (flow * k_ref[...].astype(F32)).astype(BF16)

    @pl.when(pl.program_id(0) == 0)
    def _():
        owners = g_ref.shape[0]
        keep = (iota((owners * 16, BLK), 1) % 16) == (iota((owners * 16, BLK), 0) % 16)
        by_pole = ((iota((BLK, POLES), 0) // 16) == iota((BLK, POLES), 1)).astype(BF16)
        for n, out in ((0, gr_ref), (1, gl_ref)):
            wide = jnp.broadcast_to(g_ref[:, n : n + 1, :], (owners, 16, BLK)).reshape(owners * 16, BLK)
            wide = jnp.where(keep, wide, 0.0)
            hi = wide.astype(BF16)
            mid = (wide - hi.astype(F32)).astype(BF16)
            low = (wide - hi.astype(F32) - mid.astype(F32)).astype(BF16)
            out[...] = dot(hi, by_pole) + dot(mid, by_pole) + dot(low, by_pole)
        gs_ref[...] = g_ref[:, 2, :]


def finish(z, f, cotangent, key_input, value_input, rows):
    width = z.shape[1]
    tile = 512
    owners = rows.shape[0]
    col = pl.BlockSpec((TOK, tile), lambda i: (0, i))

    def whole(shape):
        return pl.BlockSpec(shape, lambda i: (0,) * len(shape))

    return pl.pallas_call(
        finish_kernel,
        grid=(width // tile,),
        out_shape=(
            *[jax.ShapeDtypeStruct((TOK, width), BF16)] * 3,
            jax.ShapeDtypeStruct((owners * 16, POLES), F32),
            jax.ShapeDtypeStruct((owners * 16, POLES), F32),
            jax.ShapeDtypeStruct((owners, BLK), F32),
        ),
        in_specs=[col] * 5 + [whole(rows.shape)],
        out_specs=(col, col, col, whole((owners * 16, POLES)), whole((owners * 16, POLES)), whole((owners, BLK))),
        name="finish",
    )(z, f, cotangent, key_input, value_input, rows)


def local(queries, key_input, value_input, cotangent, residues, log_rates, skip_gain):
    z, f, rows = exchange(
        queries, key_input, value_input, cotangent, residues, log_rates, skip_gain.reshape(1, -1)
    )
    gq, gk, gv, gr, gl, gs = finish(z, f, cotangent, key_input, value_input, rows)
    return (gq, gk, gv, gr, gl, gs.reshape(-1))


def solution(mesh):
    placed = (P("ctx", "ch"), P("ctx", "ch"), P("ctx", "ch"), P("ctx", "ch"), P(), P(), P())
    return jax.shard_map(
        local,
        mesh=mesh,
        in_specs=placed,
        out_specs=(P("ctx", "ch"), P("ctx", "ch"), P("ctx", "ch"), P(), P(), P()),
        check_vma=False,
    )
```

```python
import functools
import math

import jax
import jax.numpy as jnp
from jax import lax
from jax.experimental import pallas as pl
from jax.experimental.pallas import tpu as pltpu
from jax.sharding import PartitionSpec as P

GROUP = 16
POLES = 16
OWN = 8
BLK = 256
TOK = 128

MESH = pl.DeviceIdType.MESH
F32 = jnp.float32
BF16 = jnp.bfloat16
HIGHEST = lax.Precision.HIGHEST


def iota(shape, dim):
    return lax.broadcasted_iota(jnp.int32, shape, dim)


def dot(a, b, dims=((1,), (0,)), precision=None):
    return lax.dot_general(
        a, b, (dims, ((), ())), precision=precision, preferred_element_type=F32
    )


def comm_kernel(
    nsb, nch,
    q_hbm, k_hbm, v_hbm, c_hbm, res_hbm, log_hbm, skip_hbm,
    gq_ref, gk_ref, gv_ref, gr_ref, gl_ref, gs_ref,
    q_ref, k_ref, v_ref, c_ref, in_sem, log_ref, res_ref, skip_ref, par_sem, lam_s, res_s,
    x_s, d_s, ed_s, el_s, ed2_s, el2_s, h_s, hr_s, zl_s, fl_s,
    p1s, p1r, p2s, p2r, p3s, p3r, pbs, pbr, p4s, p4r, p5s, p5r,
    s1, r1, s2, r2, s3, r3, sb_, rb_, s4, r4, s5, r5,
):
    ctx = lax.axis_index("ctx")
    ch = lax.axis_index("ch")
    own = ctx % OWN
    sup = ctx // OWN

    def load(i, n):
        cols = pl.ds(pl.multiple_of(i * BLK, BLK), BLK)
        src, dst = ((q_hbm, q_ref), (k_hbm, k_ref), (v_hbm, v_ref), (c_hbm, c_ref))[n]
        return pltpu.make_async_copy(src.at[:, cols], dst.at[:, cols], in_sem.at[i, n])

    shard = pl.ds(pl.multiple_of(ch * TOK, TOK), TOK)
    wide_shard = pl.ds(pl.multiple_of(ch * (OWN * BLK), OWN * BLK), OWN * BLK)
    params = [
        pltpu.make_async_copy(log_hbm.at[:, shard], log_ref, par_sem.at[0]),
        pltpu.make_async_copy(res_hbm.at[:, shard], res_ref, par_sem.at[1]),
        pltpu.make_async_copy(skip_hbm.at[:, wide_shard], skip_ref, par_sem.at[2]),
    ]
    for copy in params:
        copy.start()

    @pl.loop(0, OWN)
    def _(i):
        for n in range(4):
            load(i, n).start()

    barrier = pltpu.get_barrier_semaphore()

    def greet(ctx_to, ch_to):
        pl.semaphore_signal(barrier, inc=1, device_id=(ctx_to, ch_to), device_id_type=MESH)

    @pl.loop(1, OWN)
    def _(j):
        greet(sup * OWN + (own + j) % OWN, ch)

    @pl.loop(1, nsb)
    def _(j):
        greet(((sup + j) % nsb) * OWN + own, ch)

    @pl.loop(1, nch)
    def _(i):
        @pl.loop(0, OWN)
        def _(j):
            greet(sup * OWN + j, (ch + i) % nch)

    lane_t = iota((GROUP, TOK), 1).astype(F32)
    same_group = (iota((BLK, BLK), 0) % 16) == (iota((BLK, BLK), 1) // 16)
    pick_pole = ((iota((POLES, BLK), 1) // 16) == iota((POLES, BLK), 0)).astype(BF16)
    spread_pole = ((iota((BLK, POLES), 0) // 16) == iota((BLK, POLES), 1)).astype(BF16)

    for copy in params:
        copy.wait()
    lam_s[...] = jnp.exp(log_ref[...]).T
    res_s[...] = res_ref[...].T

    @pl.loop(0, OWN)
    def _(i):
        rows = pl.ds(pl.multiple_of(i * 16, 16), 16)
        lam = lam_s[rows, :]
        res = res_s[rows, :]
        taps = jnp.zeros((GROUP, TOK), F32)
        back = jnp.zeros((GROUP, TOK), F32)
        for p in range(POLES):
            lam_p = lam[:, p : p + 1]
            res_p = res[:, p : p + 1]
            ed = jnp.exp(-lam_p * lane_t)
            el = jnp.exp(-lam_p * (TOK - 1.0 - lane_t))
            at = pl.ds(p * 16, 16)
            ed_s[i, at, :] = ed.astype(BF16)
            el_s[i, at, :] = el.astype(BF16)
            ed2_s[i, at, :] = (ed * (lane_t + 1.0)).astype(BF16)
            el2_s[i, at, :] = (el * (TOK - 1.0 - lane_t)).astype(BF16)
            taps = taps + res_p * ed
            back = back + (res_p * jnp.exp(-lam_p)) * el
        h_s[i] = taps
        hr_s[i] = jnp.where(lane_t == 0.0, taps, back)

    @pl.loop(0, OWN)
    def _(i):
        cols = pl.ds(pl.multiple_of(i * BLK, BLK), BLK)
        for n in range(4):
            load(i, n).wait()
        x = (k_ref[:, cols].astype(F32) * v_ref[:, cols].astype(F32)).astype(BF16)
        d = (c_ref[:, cols].astype(F32) * q_ref[:, cols].astype(F32)).astype(BF16)
        x_s[:, cols] = x
        d_s[:, cols] = d
        pbs[i, 2:3, :] = jnp.sum(x.astype(F32) * d.astype(F32), axis=0, keepdims=True)
        for n, (table, val) in enumerate(((el_s, x), (ed_s, d), (el2_s, x), (ed2_s, d))):
            full = dot(table[i], val)
            full = jnp.where(same_group, full, 0.0).astype(BF16)
            p1s[i, n] = dot(pick_pole, full).astype(BF16)

    pl.semaphore_wait(barrier, (OWN - 1) + (nsb - 1) + (nch - 1) * OWN)

    def to_own(j, src, dst, send, recv):
        other = (own + j) % OWN
        return pltpu.make_async_remote_copy(
            src_ref=src.at[other], dst_ref=dst.at[own], send_sem=send.at[other], recv_sem=recv.at[own],
            device_id=(sup * OWN + other, ch), device_id_type=MESH,
        )

    def from_own(j, src, dst, send, recv):
        other = (own + j) % OWN
        return pltpu.make_async_remote_copy(
            src_ref=src.at[other], dst_ref=dst.at[other], send_sem=send.at[other], recv_sem=recv.at[other],
            device_id=(sup * OWN + other, ch), device_id_type=MESH,
        )

    def send_own(*args):
        @pl.loop(1, OWN)
        def _(j):
            to_own(j, *args).start()

    def wait_own(*args):
        @pl.loop(1, OWN)
        def _(j):
            from_own(j, *args).wait_recv()

    def sent_own(*args):
        @pl.loop(1, OWN)
        def _(j):
            from_own(j, *args).wait_send()

    send_own(p1s, p1r, s1, r1)
    p1r[own] = p1s[own]
    p2r[sup] = jnp.zeros((POLES, BLK), BF16)

    row_t = iota((TOK, TOK), 0)
    col_t = iota((TOK, TOK), 1)
    lane_group = iota((TOK, BLK), 1) // 16

    @pl.loop(0, OWN)
    def _(i):
        cols = pl.ds(pl.multiple_of(i * BLK, BLK), BLK)
        x = x_s[:, cols]
        acc = jnp.zeros((TOK, BLK), F32)
        hr = hr_s[i]
        for g in range(16):
            wide = jnp.broadcast_to(hr[g : g + 1, :], (TOK, TOK))
            mat = pltpu.roll(wide, 0, 1, stride=1, stride_axis=0)
            mat = jnp.where(col_t <= row_t, mat, 0.0).astype(BF16)
            acc = jnp.where(lane_group == g, dot(mat, x), acc)
        zl_s[:, cols] = acc

    rows = pl.ds(pl.multiple_of(own * 16, 16), 16)
    lam_own = lam_s[rows, :]
    res_own = res_s[rows, :]
    to_chan = ((iota((16, BLK), 1) // 16) == iota((16, BLK), 0)).astype(F32)
    lam_pc = dot(lam_own, to_chan, ((0,), (0,)), HIGHEST)
    res_pc = dot(res_own, to_chan, ((0,), (0,)), HIGHEST)
    w = jnp.exp(-float(TOK) * lam_pc)
    e1 = jnp.exp(-lam_pc)
    re1 = res_pc * e1

    wait_own(p1s, p1r, s1, r1)
    sum_l = jnp.zeros((POLES, BLK), F32)
    sum_d = jnp.zeros((POLES, BLK), F32)
    for b in range(OWN):
        sum_l = w * sum_l + p1r[b, 0].astype(F32)
        sum_d = w * sum_d + p1r[OWN - 1 - b, 1].astype(F32)
    p2s[0] = sum_l.astype(BF16)
    p2s[1] = sum_d.astype(BF16)

    def sup_copy(j, slot):
        other = (sup + j) % nsb
        later = (other > sup).astype(jnp.int32)
        return pltpu.make_async_remote_copy(
            src_ref=p2s.at[1 - later], dst_ref=p2r.at[slot], send_sem=s2.at[other], recv_sem=r2.at[slot],
            device_id=(other * OWN + own, ch), device_id_type=MESH,
        )

    @pl.loop(1, nsb)
    def _(j):
        sup_copy(j, sup).start()

    lane_row = iota((16, BLK), 1)
    diag = (lane_row % 16) == iota((16, BLK), 0)
    flip = (row_t == TOK - 1 - col_t).astype(BF16)

    @pl.loop(0, OWN)
    def _(i):
        cols = pl.ds(pl.multiple_of(i * BLK, BLK), BLK)
        x = dot(flip, x_s[:, cols]).astype(BF16)
        d = d_s[:, cols]
        sums = []
        for g in range(16):
            dm = jnp.where(lane_group == g, d, jnp.zeros_like(d))
            corr = dot(x, dm, ((1,), (1,)))
            corr = jnp.where(col_t >= TOK - 1 - row_t, corr, 0.0)
            corr = pltpu.roll(corr, 1, 1, stride=1, stride_axis=0)
            sums.append(jnp.sum(corr, axis=0, keepdims=True))
        fg = jnp.concatenate(sums, axis=0)
        hi = fg.astype(BF16)
        lo = (fg - hi.astype(F32)).astype(BF16)
        both = jnp.concatenate([hi, lo], axis=0)
        r_in = dot(both, ed_s[i], ((1,), (1,)))
        m_in = dot(both, ed2_s[i], ((1,), (1,)))
        r_in = r_in[:16] + r_in[16:]
        m_in = m_in[:16] + m_in[16:] - r_in
        pbs[i, 0:1, :] = jnp.sum(jnp.where(diag, r_in, 0.0), axis=0, keepdims=True)
        pbs[i, 1:2, :] = jnp.sum(jnp.where(diag, m_in, 0.0), axis=0, keepdims=True)
        pbs[i, 3:4, :] = jnp.zeros((1, BLK), F32)

    send_own(pbs, pbr, sb_, rb_)
    pbr[own] = pbs[own]

    @pl.loop(0, OWN)
    def _(i):
        cols = pl.ds(pl.multiple_of(i * BLK, BLK), BLK)
        d = d_s[:, cols]
        acc = jnp.zeros((TOK, BLK), F32)
        h = h_s[i]
        for g in range(16):
            wide = jnp.broadcast_to(h[g : g + 1, :], (TOK, TOK))
            mat = pltpu.roll(wide, 0, 1, stride=1, stride_axis=0)
            mat = jnp.where(col_t >= row_t, mat, 0.0).astype(BF16)
            acc = jnp.where(lane_group == g, dot(mat, d), acc)
        fl_s[:, cols] = acc

    @pl.loop(1, nsb)
    def _(j):
        sup_copy(j, (sup + j) % nsb).wait_recv()

    in_s = jnp.zeros((POLES, BLK), F32)
    in_f = jnp.zeros((POLES, BLK), F32)
    for b in range(nsb):
        gap = jnp.maximum(jnp.abs(sup - b) - 1, 0).astype(F32) * float(TOK * OWN)
        term = jnp.exp(-lam_pc * gap) * p2r[b].astype(F32)
        in_s = in_s + jnp.where(b < sup, term, 0.0)
        in_f = in_f + jnp.where(b > sup, term, 0.0)
    carry_s = []
    for b in range(OWN):
        carry_s.append(in_s)
        p3s[b, 0] = (re1 * in_s).astype(BF16)
        in_s = w * in_s + p1r[b, 0].astype(F32)
    r_sum = jnp.zeros((POLES, BLK), F32)
    m_sum = jnp.zeros((POLES, BLK), F32)
    for b in reversed(range(OWN)):
        p3s[b, 1] = (re1 * in_f).astype(BF16)
        d_b = p1r[b, 1].astype(F32)
        r_sum = r_sum + d_b * carry_s[b]
        m_sum = (
            m_sum
            + p1r[b, 3].astype(F32) * carry_s[b]
            + p1r[b, 2].astype(F32) * in_f
            + (float(TOK) * w) * (carry_s[b] * in_f)
        )
        in_f = w * in_f + d_b
    send_own(p3s, p3r, s3, r3)
    p3r[own] = p3s[own]

    chan_group = ((iota((BLK, BLK), 0) // 16) == (iota((BLK, BLK), 1) % 16)).astype(F32)
    pole_row = (iota((POLES, BLK), 1) // 16) == iota((POLES, BLK), 0)
    sums = dot(jnp.concatenate([r_sum * e1, m_sum * e1], axis=0), chan_group, precision=HIGHEST)
    r_row = jnp.sum(jnp.where(pole_row, sums[:POLES], 0.0), axis=0, keepdims=True)
    m_row = jnp.sum(jnp.where(pole_row, sums[POLES:], 0.0), axis=0, keepdims=True)
    wait_own(pbs, pbr, sb_, rb_)
    part = pbr[0]
    for b in range(1, OWN):
        part = part + pbr[b]
    p4s[0:1, :] = part[0:1] + r_row
    p4s[1:2, :] = part[1:2] + m_row
    p4s[2:4, :] = part[2:4]

    def grad_copy(j, slot):
        other = (sup + j) % nsb
        return pltpu.make_async_remote_copy(
            src_ref=p4s, dst_ref=p4r.at[slot], send_sem=s4.at[other], recv_sem=r4.at[slot],
            device_id=(other * OWN + own, ch), device_id_type=MESH,
        )

    @pl.loop(1, nsb)
    def _(j):
        grad_copy(j, sup).start()

    p4r[sup] = p4s[...]

    wait_own(p3s, p3r, s3, r3)

    @pl.loop(0, OWN)
    def _(i):
        cols = pl.ds(pl.multiple_of(i * BLK, BLK), BLK)
        skip = skip_ref[:, cols]
        both = []
        for n, (table, src, loc) in enumerate(((ed_s, x_s, zl_s), (el_s, d_s, fl_s))):
            wide = dot(spread_pole, p3r[i, n])
            wide = jnp.where(same_group, wide, 0.0).astype(BF16)
            corr = dot(table[i], wide, ((0,), (0,)))
            out = skip * src[:, cols].astype(F32) + (loc[:, cols] + corr)
            both.append(out.astype(BF16).astype(F32))
        hidden, flow = both
        gq_ref[:, cols] = (c_ref[:, cols].astype(F32) * hidden).astype(BF16)
        gk_ref[:, cols] = (flow * v_ref[:, cols].astype(F32)).astype(BF16)
        gv_ref[:, cols] = (flow * k_ref[:, cols].astype(F32)).astype(BF16)

    to_pole = ((iota((POLES, BLK), 1) // 16) == iota((POLES, BLK), 0)).astype(F32)
    scale = dot(-lam_own * res_own, to_pole, precision=HIGHEST)
    scale_row = jnp.sum(jnp.where(diag, scale, 0.0), axis=0, keepdims=True)
    length = float(TOK * OWN * nsb)

    @pl.loop(1, nsb)
    def _(j):
        grad_copy(j, (sup + j) % nsb).wait_recv()

    total = p4r[0]
    for b in range(1, nsb):
        total = total + p4r[b]
    p5s[0:1, :] = total[0:1] / length
    p5s[1:2, :] = total[1:2] * scale_row / math.sqrt(length)
    p5s[2:4, :] = total[2:4] / math.sqrt(length)

    def last_copy(i, j, mine):
        ch_to = (ch + i) % nch
        own_to = (own + j) % OWN
        here = ch * OWN + own
        there = ch_to * OWN + own_to
        slot = here if mine else there
        return pltpu.make_async_remote_copy(
            src_ref=p5s, dst_ref=p5r.at[slot], send_sem=s5.at[there], recv_sem=r5.at[slot],
            device_id=(sup * OWN + own_to, ch_to), device_id_type=MESH,
        )

    @pl.loop(1, nch * OWN)
    def _(n):
        last_copy(n // OWN, n % OWN, True).start()

    p5r[ch * OWN + own] = p5s[...]

    sent_own(p1s, p1r, s1, r1)
    sent_own(pbs, pbr, sb_, rb_)
    sent_own(p3s, p3r, s3, r3)

    @pl.loop(1, nsb)
    def _(j):
        sup_copy(j, sup).wait_send()
        grad_copy(j, sup).wait_send()

    @pl.loop(1, nch * OWN)
    def _(n):
        last_copy(n // OWN, n % OWN, False).wait_recv()

    @pl.loop(1, nch * OWN)
    def _(n):
        last_copy(n // OWN, n % OWN, True).wait_send()

    place = (
        (iota((OWN * BLK, TOK), 0) // BLK == iota((OWN * BLK, TOK), 1) // 16)
        & (iota((OWN * BLK, TOK), 0) % 16 == iota((OWN * BLK, TOK), 1) % 16)
    ).astype(BF16)
    keep = (iota((POLES, OWN * BLK), 1) % BLK) // 16 == iota((POLES, OWN * BLK), 0)
    for i in range(nch):
        parts = []
        for n in range(2):
            row = jnp.concatenate([p5r[i * OWN + j, n : n + 1, :] for j in range(OWN)], axis=1)
            hi = row.astype(BF16).astype(F32)
            mid = (row - hi).astype(BF16).astype(F32)
            for piece in (hi, mid, row - hi - mid):
                parts.append(jnp.where(keep, jnp.broadcast_to(piece, keep.shape), 0.0).astype(BF16))
        got = dot(jnp.concatenate(parts, axis=0), place)
        for n, out in enumerate((gr_ref, gl_ref)):
            at = n * 3 * POLES
            out[:, i * TOK : (i + 1) * TOK] = (
                got[at : at + POLES] + got[at + POLES : at + 2 * POLES] + got[at + 2 * POLES : at + 3 * POLES]
            )
        for j in range(OWN):
            n = i * OWN + j
            gs_ref[:, n * BLK : (n + 1) * BLK] = p5r[n, 2:3, :]


def exchange(queries, key_input, value_input, cotangent, residues, log_rates, skip_row):
    nsb = lax.axis_size("ctx") // OWN
    nch = lax.axis_size("ch")
    width = OWN * BLK
    vmem = pl.BlockSpec(memory_space=pltpu.VMEM)
    dma = pltpu.SemaphoreType.DMA
    state = (POLES, BLK)
    return pl.pallas_call(
        functools.partial(comm_kernel, nsb, nch),
        out_shape=(
            *[jax.ShapeDtypeStruct((TOK, width), BF16)] * 3,
            *[jax.ShapeDtypeStruct((POLES, nch * TOK), F32)] * 2,
            jax.ShapeDtypeStruct((1, nch * width), F32),
        ),
        in_specs=[pl.BlockSpec(memory_space=pltpu.HBM)] * 7,
        out_specs=(vmem,) * 6,
        scratch_shapes=[
            *[pltpu.VMEM((TOK, width), BF16)] * 4,
            dma((OWN, 4)),
            pltpu.VMEM((POLES, TOK), F32),
            pltpu.VMEM((POLES, TOK), F32),
            pltpu.VMEM((1, width), F32),
            dma((3,)),
            pltpu.VMEM((TOK, POLES), F32),
            pltpu.VMEM((TOK, POLES), F32),
            pltpu.VMEM((TOK, width), BF16),
            pltpu.VMEM((TOK, width), BF16),
            *[pltpu.VMEM((OWN, BLK, TOK), BF16)] * 4,
            pltpu.VMEM((OWN, GROUP, TOK), F32),
            pltpu.VMEM((OWN, GROUP, TOK), F32),
            pltpu.VMEM((TOK, width), F32),
            pltpu.VMEM((TOK, width), F32),
            pltpu.VMEM((OWN, 4) + state, BF16),
            pltpu.VMEM((OWN, 4) + state, BF16),
            pltpu.VMEM((2,) + state, BF16),
            pltpu.VMEM((nsb,) + state, BF16),
            pltpu.VMEM((OWN, 2) + state, BF16),
            pltpu.VMEM((OWN, 2) + state, BF16),
            pltpu.VMEM((OWN, 4, BLK), F32),
            pltpu.VMEM((OWN, 4, BLK), F32),
            pltpu.VMEM((4, BLK), F32),
            pltpu.VMEM((nsb, 4, BLK), F32),
            pltpu.VMEM((4, BLK), F32),
            pltpu.VMEM((nch * OWN, 4, BLK), F32),
            dma((OWN,)), dma((OWN,)),
            dma((nsb,)), dma((nsb,)),
            dma((OWN,)), dma((OWN,)),
            dma((OWN,)), dma((OWN,)),
            dma((nsb,)), dma((nsb,)),
            dma((nch * OWN,)), dma((nch * OWN,)),
        ],
        compiler_params=pltpu.CompilerParams(
            collective_id=0, has_side_effects=True, vmem_limit_bytes=48 << 20
        ),
        name="exchange",
    )(
        *[
            pltpu.with_memory_space_constraint(val, pltpu.HBM)
            for val in (queries, key_input, value_input, cotangent, residues, log_rates, skip_row)
        ]
    )


def store_kernel(*refs):
    count = (len(refs) - 1) // 2
    sem = refs[-1]
    copies = [pltpu.make_async_copy(refs[n], refs[count + n], sem.at[n]) for n in range(count)]
    for copy in copies:
        copy.start()
    for copy in copies:
        copy.wait()


def store(*arrays):
    count = len(arrays)
    return pl.pallas_call(
        store_kernel,
        out_shape=tuple(jax.ShapeDtypeStruct(val.shape, val.dtype) for val in arrays),
        in_specs=[pl.BlockSpec(memory_space=pltpu.VMEM)] * count,
        out_specs=(pl.BlockSpec(memory_space=pltpu.HBM),) * count,
        scratch_shapes=[pltpu.SemaphoreType.DMA((count,))],
        compiler_params=pltpu.CompilerParams(vmem_limit_bytes=1 << 20),
        name="store",
    )(*arrays)


def local(queries, key_input, value_input, cotangent, residues, log_rates, skip_gain):
    gq, gk, gv, gr, gl, gs = store(*exchange(
        queries, key_input, value_input, cotangent, residues.T, log_rates.T, skip_gain.reshape(1, -1)
    ))
    return (gq, gk, gv, gr.T, gl.T, gs.reshape(-1))


def solution(mesh):
    placed = (P("ctx", "ch"), P("ctx", "ch"), P("ctx", "ch"), P("ctx", "ch"), P(), P(), P())
    return jax.shard_map(
        local,
        mesh=mesh,
        in_specs=placed,
        out_specs=(P("ctx", "ch"), P("ctx", "ch"), P("ctx", "ch"), P(), P(), P()),
        check_vma=False,
    )
```

```python
import functools
import math

import jax
import jax.numpy as jnp
from jax import lax
from jax.experimental import pallas as pl
from jax.experimental.pallas import tpu as pltpu
from jax.sharding import PartitionSpec as P

GROUP = 16
POLES = 16
OWN = 8
BLK = 256
TOK = 128

MESH = pl.DeviceIdType.MESH
F32 = jnp.float32
BF16 = jnp.bfloat16
HIGHEST = lax.Precision.HIGHEST


def iota(shape, dim):
    return lax.broadcasted_iota(jnp.int32, shape, dim)


def dot(a, b, dims=((1,), (0,)), precision=None):
    return lax.dot_general(
        a, b, (dims, ((), ())), precision=precision, preferred_element_type=F32
    )


def comm_kernel(
    nsb, nch,
    q_hbm, k_hbm, v_hbm, c_hbm, res_hbm, log_hbm, skip_hbm,
    gq_ref, gk_ref, gv_ref, gr_ref, gl_ref, gs_ref,
    q_ref, k_ref, v_ref, c_ref, in_sem, log_ref, res_ref, skip_ref, par_sem, lam_s, res_s,
    x_s, d_s, ed_s, el_s, ed2_s, el2_s, h_s, hr_s, zl_s, fl_s,
    p1s, p1r, pms, pmr, p2s, p2r, p3s, p3r, pbs, pbr, p4s, p4r, p5s, p5r, coef_s, place_s, swap_s, swap_r, sh,
    s1, r1, sm, rm, s2, r2, s3, r3, sb_, rb_, s4, r4, s5, r5,
):
    ctx = lax.axis_index("ctx")
    ch = lax.axis_index("ch")
    own = ctx % OWN
    sup = ctx // OWN

    def load(i, n):
        cols = pl.ds(pl.multiple_of(i * BLK, BLK), BLK)
        src, dst = ((q_hbm, q_ref), (k_hbm, k_ref), (v_hbm, v_ref), (c_hbm, c_ref))[n]
        return pltpu.make_async_copy(src.at[:, cols], dst.at[:, cols], in_sem.at[i, n])

    shard = pl.ds(pl.multiple_of(ch * TOK, TOK), TOK)
    wide_shard = pl.ds(pl.multiple_of(ch * (OWN * BLK), OWN * BLK), OWN * BLK)
    params = [
        pltpu.make_async_copy(log_hbm.at[:, shard], log_ref, par_sem.at[0]),
        pltpu.make_async_copy(res_hbm.at[:, shard], res_ref, par_sem.at[1]),
        pltpu.make_async_copy(skip_hbm.at[:, wide_shard], skip_ref, par_sem.at[2]),
    ]
    for copy in params:
        copy.start()

    @pl.loop(0, OWN)
    def _(i):
        for n in range(4):
            load(i, n).start()

    barrier = pltpu.get_barrier_semaphore()

    def greet(ctx_to, ch_to):
        pl.semaphore_signal(barrier, inc=1, device_id=(ctx_to, ch_to), device_id_type=MESH)

    @pl.loop(1, OWN)
    def _(j):
        greet(sup * OWN + (own + j) % OWN, ch)

    @pl.loop(1, nsb)
    def _(j):
        greet(((sup + j) % nsb) * OWN + own, ch)

    @pl.loop(1, nch)
    def _(i):
        @pl.loop(0, OWN)
        def _(j):
            greet(sup * OWN + j, (ch + i) % nch)

    lane_t = iota((GROUP, TOK), 1).astype(F32)
    same_group = (iota((BLK, BLK), 0) % 16) == (iota((BLK, BLK), 1) // 16)
    pick_pole = ((iota((POLES, BLK), 1) // 16) == iota((POLES, BLK), 0)).astype(BF16)
    spread_pole = ((iota((BLK, POLES), 0) // 16) == iota((BLK, POLES), 1)).astype(BF16)

    for copy in params:
        copy.wait()
    lam_s[...] = jnp.exp(log_ref[...]).T
    res_s[...] = res_ref[...].T

    @pl.loop(0, OWN)
    def _(i):
        rows = pl.ds(pl.multiple_of(i * 16, 16), 16)
        lam = lam_s[rows, :]
        res = res_s[rows, :]
        taps = jnp.zeros((GROUP, TOK), F32)
        back = jnp.zeros((GROUP, TOK), F32)
        for p in range(POLES):
            lam_p = lam[:, p : p + 1]
            res_p = res[:, p : p + 1]
            ed = jnp.exp(-lam_p * lane_t)
            el = jnp.exp(-lam_p * (TOK - 1.0 - lane_t))
            at = pl.ds(p * 16, 16)
            ed_s[i, at, :] = ed.astype(BF16)
            el_s[i, at, :] = el.astype(BF16)
            ed2_s[i, at, :] = (ed * (lane_t + 1.0)).astype(BF16)
            el2_s[i, at, :] = (el * (TOK - 1.0 - lane_t)).astype(BF16)
            taps = taps + res_p * ed
            back = back + (res_p * jnp.exp(-lam_p)) * el
        h_s[i] = taps
        hr_s[i] = jnp.where(lane_t == 0.0, taps, back)

    @pl.loop(0, OWN)
    def _(i):
        cols = pl.ds(pl.multiple_of(i * BLK, BLK), BLK)
        for n in range(4):
            load(i, n).wait()
        x = (k_ref[:, cols].astype(F32) * v_ref[:, cols].astype(F32)).astype(BF16)
        d = (c_ref[:, cols].astype(F32) * q_ref[:, cols].astype(F32)).astype(BF16)
        x_s[:, cols] = x
        d_s[:, cols] = d
        pbs[i, 2:3, :] = jnp.sum(x.astype(F32) * d.astype(F32), axis=0, keepdims=True)
        for n, (table, val) in enumerate(((el_s, x), (ed_s, d), (el2_s, x), (ed2_s, d))):
            full = dot(table[i], val)
            full = jnp.where(same_group, full, 0.0).astype(BF16)
            kept = dot(pick_pole, full).astype(BF16)
            if n < 2:
                p1s[i, n] = kept
            else:
                pms[i, n - 2] = kept

    pl.semaphore_wait(barrier, (OWN - 1) + (nsb - 1) + (nch - 1) * OWN)

    def to_own(j, src, dst, send, recv):
        other = (own + j) % OWN
        return pltpu.make_async_remote_copy(
            src_ref=src.at[other], dst_ref=dst.at[own], send_sem=send.at[other], recv_sem=recv.at[own],
            device_id=(sup * OWN + other, ch), device_id_type=MESH,
        )

    def from_own(j, src, dst, send, recv):
        other = (own + j) % OWN
        return pltpu.make_async_remote_copy(
            src_ref=src.at[other], dst_ref=dst.at[other], send_sem=send.at[other], recv_sem=recv.at[other],
            device_id=(sup * OWN + other, ch), device_id_type=MESH,
        )

    def send_own(*args):
        @pl.loop(1, OWN)
        def _(j):
            to_own(j, *args).start()

    def wait_own(*args):
        @pl.loop(1, OWN)
        def _(j):
            from_own(j, *args).wait_recv()

    def sent_own(*args):
        @pl.loop(1, OWN)
        def _(j):
            from_own(j, *args).wait_send()

    send_own(p1s, p1r, s1, r1)
    send_own(pms, pmr, sm, rm)
    p1r[own] = p1s[own]
    pmr[own] = pms[own]

    row_t = iota((TOK, TOK), 0)
    col_t = iota((TOK, TOK), 1)
    lane_group = iota((TOK, BLK), 1) // 16

    lane_row = iota((16, BLK), 1)
    diag = (lane_row % 16) == iota((16, BLK), 0)
    flip = (row_t == TOK - 1 - col_t).astype(BF16)

    @pl.loop(0, OWN)
    def _(i):
        cols = pl.ds(pl.multiple_of(i * BLK, BLK), BLK)
        x = dot(flip, x_s[:, cols]).astype(BF16)
        d = d_s[:, cols]
        sums = []
        for g in range(16):
            dm = jnp.where(lane_group == g, d, jnp.zeros_like(d))
            corr = dot(x, dm, ((1,), (1,)))
            corr = jnp.where(col_t >= TOK - 1 - row_t, corr, 0.0)
            corr = pltpu.roll(corr, 1, 1, stride=1, stride_axis=0)
            sums.append(jnp.sum(corr, axis=0, keepdims=True))
        fg = jnp.concatenate(sums, axis=0)
        hi = fg.astype(BF16)
        lo = (fg - hi.astype(F32)).astype(BF16)
        both = jnp.concatenate([hi, lo], axis=0)
        r_in = dot(both, ed_s[i], ((1,), (1,)))
        m_in = dot(both, ed2_s[i], ((1,), (1,)))
        r_in = r_in[:16] + r_in[16:]
        m_in = m_in[:16] + m_in[16:] - r_in
        pbs[i, 0:1, :] = jnp.sum(jnp.where(diag, r_in, 0.0), axis=0, keepdims=True)
        pbs[i, 1:2, :] = jnp.sum(jnp.where(diag, m_in, 0.0), axis=0, keepdims=True)
        pbs[i, 3:4, :] = jnp.zeros((1, BLK), F32)

    send_own(pbs, pbr, sb_, rb_)
    pbr[own] = pbs[own]

    rows = pl.ds(pl.multiple_of(own * 16, 16), 16)
    lam_own = lam_s[rows, :]
    res_own = res_s[rows, :]
    to_chan = ((iota((16, BLK), 1) // 16) == iota((16, BLK), 0)).astype(F32)
    lam_pc = dot(lam_own, to_chan, ((0,), (0,)), HIGHEST)
    res_pc = dot(res_own, to_chan, ((0,), (0,)), HIGHEST)
    w = jnp.exp(-float(TOK) * lam_pc)
    e1 = jnp.exp(-lam_pc)
    re1 = res_pc * e1

    wait_own(p1s, p1r, s1, r1)
    sum_l = jnp.zeros((POLES, BLK), F32)
    sum_d = jnp.zeros((POLES, BLK), F32)
    for b in range(OWN):
        sum_l = w * sum_l + p1r[b, 0].astype(F32)
        sum_d = w * sum_d + p1r[OWN - 1 - b, 1].astype(F32)
    p2s[0] = sum_l.astype(BF16)
    p2s[1] = sum_d.astype(BF16)

    col = sup // 2
    half = sup % 2
    ncol = nsb // 2

    def col_copy(j, slot):
        other = (col + j) % ncol
        later = (other > col).astype(jnp.int32)
        return pltpu.make_async_remote_copy(
            src_ref=p2s.at[1 - later], dst_ref=p2r.at[slot], send_sem=s2.at[other], recv_sem=r2.at[slot],
            device_id=((other * 2 + half) * OWN + own, ch), device_id_type=MESH,
        )

    def half_copy():
        return pltpu.make_async_remote_copy(
            src_ref=swap_s, dst_ref=swap_r, send_sem=sh.at[0], recv_sem=sh.at[1],
            device_id=((col * 2 + 1 - half) * OWN + own, ch), device_id_type=MESH,
        )

    @pl.loop(1, ncol)
    def _(j):
        col_copy(j, col).start()

    scale = dot(
        -lam_own * res_own, ((iota((POLES, BLK), 1) // 16) == iota((POLES, BLK), 0)).astype(F32), precision=HIGHEST
    )
    scale_row = jnp.sum(jnp.where(diag, scale, 0.0), axis=0, keepdims=True)

    @pl.loop(0, ncol)
    def _(b):
        gap = jnp.maximum(jnp.abs(col - b) - 1, 0).astype(F32) * float(TOK * OWN * 2)
        coef_s[b] = jnp.exp(-lam_pc * gap)

    wide_w = jnp.exp(-float(TOK * OWN) * lam_pc)
    wide_w2 = jnp.exp(-float(TOK * OWN * 2) * lam_pc)

    place_s[...] = (
        (iota((OWN * BLK, TOK), 0) // BLK == iota((OWN * BLK, TOK), 1) // 16)
        & (iota((OWN * BLK, TOK), 0) % 16 == iota((OWN * BLK, TOK), 1) % 16)
    ).astype(BF16)
    @pl.loop(0, OWN)
    def _(i):
        cols = pl.ds(pl.multiple_of(i * BLK, BLK), BLK)
        x = x_s[:, cols]
        acc = jnp.zeros((TOK, BLK), F32)
        hr = hr_s[i]
        for g in range(16):
            wide = jnp.broadcast_to(hr[g : g + 1, :], (TOK, TOK))
            mat = pltpu.roll(wide, 0, 1, stride=1, stride_axis=0)
            mat = jnp.where(col_t <= row_t, mat, 0.0).astype(BF16)
            acc = jnp.where(lane_group == g, dot(mat, x), acc)
        zl_s[:, cols] = acc

    zero = jnp.zeros((POLES, BLK), F32)

    def gather(j, sums):
        other = (col + j) % ncol
        col_copy(j, other).wait_recv()
        term = coef_s[other] * p2r[other].astype(F32)
        later = other > col
        return sums[0] + jnp.where(later, 0.0, term), sums[1] + jnp.where(later, term, 0.0)

    col_s, col_f = lax.fori_loop(1, ncol, gather, (zero, zero))
    swap_s[0] = jnp.where(half == 0, sum_l + wide_w2 * col_s, col_s).astype(BF16)
    swap_s[1] = jnp.where(half == 0, col_f, sum_d + wide_w2 * col_f).astype(BF16)
    half_copy().start()

    @pl.loop(0, OWN)
    def _(i):
        cols = pl.ds(pl.multiple_of(i * BLK, BLK), BLK)
        d = d_s[:, cols]
        acc = jnp.zeros((TOK, BLK), F32)
        h = h_s[i]
        for g in range(16):
            wide = jnp.broadcast_to(h[g : g + 1, :], (TOK, TOK))
            mat = pltpu.roll(wide, 0, 1, stride=1, stride_axis=0)
            mat = jnp.where(col_t >= row_t, mat, 0.0).astype(BF16)
            acc = jnp.where(lane_group == g, dot(mat, d), acc)
        fl_s[:, cols] = acc

    wait_own(pms, pmr, sm, rm)
    wait_own(pbs, pbr, sb_, rb_)
    part = pbr[0]
    for b in range(1, OWN):
        part = part + pbr[b]

    half_copy().wait_recv()
    in_s = wide_w * col_s + swap_r[0].astype(F32)
    in_f = wide_w * col_f + swap_r[1].astype(F32)
    carry_s = []
    for b in range(OWN):
        carry_s.append(in_s)
        p3s[b, 0] = (re1 * in_s).astype(BF16)
        in_s = w * in_s + p1r[b, 0].astype(F32)
    r_sum = jnp.zeros((POLES, BLK), F32)
    m_sum = jnp.zeros((POLES, BLK), F32)
    for b in reversed(range(OWN)):
        p3s[b, 1] = (re1 * in_f).astype(BF16)
        d_b = p1r[b, 1].astype(F32)
        r_sum = r_sum + d_b * carry_s[b]
        m_sum = (
            m_sum
            + pmr[b, 1].astype(F32) * carry_s[b]
            + pmr[b, 0].astype(F32) * in_f
            + (float(TOK) * w) * (carry_s[b] * in_f)
        )
        in_f = w * in_f + d_b
    def pack(first, second, third):
        half = BLK // 2
        top = jnp.concatenate([first, second[:, :half]], axis=1)
        low = jnp.concatenate([second[:, half:], third], axis=1)
        return jnp.concatenate([top, low], axis=0).astype(BF16)

    def unpack(val):
        half = BLK // 2
        second = jnp.concatenate([val[0:1, BLK:], val[1:2, :half]], axis=1)
        return val[0:1, :BLK], second, val[1:2, half:]

    chan_group = ((iota((BLK, BLK), 0) // 16) == (iota((BLK, BLK), 1) % 16)).astype(F32)
    pole_row = (iota((POLES, BLK), 1) // 16) == iota((POLES, BLK), 0)
    sums = dot(jnp.concatenate([r_sum * e1, m_sum * e1], axis=0), chan_group, precision=HIGHEST)
    r_row = jnp.sum(jnp.where(pole_row, sums[:POLES], 0.0), axis=0, keepdims=True)
    m_row = jnp.sum(jnp.where(pole_row, sums[POLES:], 0.0), axis=0, keepdims=True)
    p4s[...] = pack(part[0:1] + r_row, part[1:2] + m_row, part[2:3])

    def grad_copy(j, slot):
        other = (sup + j) % nsb
        return pltpu.make_async_remote_copy(
            src_ref=p4s, dst_ref=p4r.at[slot], send_sem=s4.at[other], recv_sem=r4.at[slot],
            device_id=(other * OWN + own, ch), device_id_type=MESH,
        )

    @pl.loop(1, nsb)
    def _(j):
        grad_copy(j, sup).start()

    send_own(p3s, p3r, s3, r3)
    p3r[own] = p3s[own]
    p4r[sup] = p4s[...]

    @pl.loop(0, OWN)
    def _(j):
        i = (own + j) % OWN

        @pl.when(j > 0)
        def _():
            from_own(j, p3s, p3r, s3, r3).wait_recv()

        cols = pl.ds(pl.multiple_of(i * BLK, BLK), BLK)
        skip = skip_ref[:, cols]
        both = []
        for n, (table, src, loc) in enumerate(((ed_s, x_s, zl_s), (el_s, d_s, fl_s))):
            wide = dot(spread_pole, p3r[i, n])
            wide = jnp.where(same_group, wide, 0.0).astype(BF16)
            corr = dot(table[i], wide, ((0,), (0,)))
            out = skip * src[:, cols].astype(F32) + (loc[:, cols] + corr)
            both.append(out.astype(BF16).astype(F32))
        hidden, flow = both
        gq_ref[:, cols] = (c_ref[:, cols].astype(F32) * hidden).astype(BF16)
        gk_ref[:, cols] = (flow * v_ref[:, cols].astype(F32)).astype(BF16)
        gv_ref[:, cols] = (flow * k_ref[:, cols].astype(F32)).astype(BF16)

    length = float(TOK * OWN * nsb)

    @pl.loop(1, nsb)
    def _(j):
        grad_copy(j, (sup + j) % nsb).wait_recv()

    total = p4r[0].astype(F32)
    for b in range(1, nsb):
        total = total + p4r[b].astype(F32)
    r_row, m_row, k_row = unpack(total)
    p5s[...] = pack(r_row / length, m_row * scale_row / math.sqrt(length), k_row / math.sqrt(length))

    def last_copy(i, j, mine):
        ch_to = (ch + i) % nch
        own_to = (own + j) % OWN
        here = ch * OWN + own
        there = ch_to * OWN + own_to
        slot = here if mine else there
        return pltpu.make_async_remote_copy(
            src_ref=p5s, dst_ref=p5r.at[slot], send_sem=s5.at[there], recv_sem=r5.at[slot],
            device_id=(sup * OWN + own_to, ch_to), device_id_type=MESH,
        )

    @pl.loop(1, nch * OWN)
    def _(n):
        last_copy(n // OWN, n % OWN, True).start()

    p5r[ch * OWN + own] = p5s[...]

    sent_own(p1s, p1r, s1, r1)
    sent_own(pms, pmr, sm, rm)
    sent_own(pbs, pbr, sb_, rb_)
    sent_own(p3s, p3r, s3, r3)

    half_copy().wait_send()

    @pl.loop(1, ncol)
    def _(j):
        col_copy(j, col).wait_send()

    @pl.loop(1, nsb)
    def _(j):
        grad_copy(j, sup).wait_send()

    @pl.loop(1, nch * OWN)
    def _(n):
        last_copy(n // OWN, n % OWN, False).wait_recv()

    @pl.loop(1, nch * OWN)
    def _(n):
        last_copy(n // OWN, n % OWN, True).wait_send()

    keep = (iota((POLES, OWN * BLK), 1) % BLK) // 16 == iota((POLES, OWN * BLK), 0)
    for i in range(nch):
        rows = [unpack(p5r[i * OWN + j].astype(F32)) for j in range(OWN)]
        parts = []
        for n in range(2):
            row = jnp.concatenate([val[n] for val in rows], axis=1)
            parts.append(jnp.where(keep, jnp.broadcast_to(row, keep.shape), 0.0).astype(BF16))
        got = dot(jnp.concatenate(parts, axis=0), place_s[...])
        gr_ref[:, i * TOK : (i + 1) * TOK] = got[:POLES]
        gl_ref[:, i * TOK : (i + 1) * TOK] = got[POLES:]
        for j in range(OWN):
            n = i * OWN + j
            gs_ref[:, n * BLK : (n + 1) * BLK] = rows[j][2]


def exchange(queries, key_input, value_input, cotangent, residues, log_rates, skip_row):
    nsb = lax.axis_size("ctx") // OWN
    nch = lax.axis_size("ch")
    width = OWN * BLK
    vmem = pl.BlockSpec(memory_space=pltpu.VMEM)
    dma = pltpu.SemaphoreType.DMA
    state = (POLES, BLK)
    return pl.pallas_call(
        functools.partial(comm_kernel, nsb, nch),
        out_shape=(
            *[jax.ShapeDtypeStruct((TOK, width), BF16)] * 3,
            *[jax.ShapeDtypeStruct((POLES, nch * TOK), F32)] * 2,
            jax.ShapeDtypeStruct((1, nch * width), F32),
        ),
        in_specs=[pl.BlockSpec(memory_space=pltpu.HBM)] * 7,
        out_specs=(vmem,) * 6,
        scratch_shapes=[
            *[pltpu.VMEM((TOK, width), BF16)] * 4,
            dma((OWN, 4)),
            pltpu.VMEM((POLES, TOK), F32),
            pltpu.VMEM((POLES, TOK), F32),
            pltpu.VMEM((1, width), F32),
            dma((3,)),
            pltpu.VMEM((TOK, POLES), F32),
            pltpu.VMEM((TOK, POLES), F32),
            pltpu.VMEM((TOK, width), BF16),
            pltpu.VMEM((TOK, width), BF16),
            *[pltpu.VMEM((OWN, BLK, TOK), BF16)] * 4,
            pltpu.VMEM((OWN, GROUP, TOK), F32),
            pltpu.VMEM((OWN, GROUP, TOK), F32),
            pltpu.VMEM((TOK, width), F32),
            pltpu.VMEM((TOK, width), F32),
            *[pltpu.VMEM((OWN, 2) + state, BF16)] * 4,
            pltpu.VMEM((2,) + state, BF16),
            pltpu.VMEM((nsb // 2,) + state, BF16),
            pltpu.VMEM((OWN, 2) + state, BF16),
            pltpu.VMEM((OWN, 2) + state, BF16),
            pltpu.VMEM((OWN, 4, BLK), F32),
            pltpu.VMEM((OWN, 4, BLK), F32),
            pltpu.VMEM((2, 3 * BLK // 2), BF16),
            pltpu.VMEM((nsb, 2, 3 * BLK // 2), BF16),
            pltpu.VMEM((2, 3 * BLK // 2), BF16),
            pltpu.VMEM((nch * OWN, 2, 3 * BLK // 2), BF16),
            pltpu.VMEM((nsb // 2,) + state, F32),
            pltpu.VMEM((OWN * BLK, TOK), BF16),
            pltpu.VMEM((2,) + state, BF16),
            pltpu.VMEM((2,) + state, BF16),
            dma((2,)),
            dma((OWN,)), dma((OWN,)),
            dma((OWN,)), dma((OWN,)),
            dma((nsb // 2,)), dma((nsb // 2,)),
            dma((OWN,)), dma((OWN,)),
            dma((OWN,)), dma((OWN,)),
            dma((nsb,)), dma((nsb,)),
            dma((nch * OWN,)), dma((nch * OWN,)),
        ],
        compiler_params=pltpu.CompilerParams(
            collective_id=0, has_side_effects=True, vmem_limit_bytes=48 << 20
        ),
        name="exchange",
    )(
        *[
            pltpu.with_memory_space_constraint(val, pltpu.HBM)
            for val in (queries, key_input, value_input, cotangent, residues, log_rates, skip_row)
        ]
    )


def store_kernel(*refs):
    count = (len(refs) - 1) // 2
    sem = refs[-1]
    copies = [pltpu.make_async_copy(refs[n], refs[count + n], sem.at[n]) for n in range(count)]
    for copy in copies:
        copy.start()
    for copy in copies:
        copy.wait()


def store(*arrays):
    count = len(arrays)
    return pl.pallas_call(
        store_kernel,
        out_shape=tuple(jax.ShapeDtypeStruct(val.shape, val.dtype) for val in arrays),
        in_specs=[pl.BlockSpec(memory_space=pltpu.VMEM)] * count,
        out_specs=(pl.BlockSpec(memory_space=pltpu.HBM),) * count,
        scratch_shapes=[pltpu.SemaphoreType.DMA((count,))],
        compiler_params=pltpu.CompilerParams(vmem_limit_bytes=1 << 20),
        name="store",
    )(*arrays)


def local(queries, key_input, value_input, cotangent, residues, log_rates, skip_gain):
    gq, gk, gv, gr, gl, gs = store(*exchange(
        queries, key_input, value_input, cotangent, residues.T, log_rates.T, skip_gain.reshape(1, -1)
    ))
    return (gq, gk, gv, gr.T, gl.T, gs.reshape(-1))


def solution(mesh):
    placed = (P("ctx", "ch"), P("ctx", "ch"), P("ctx", "ch"), P("ctx", "ch"), P(), P(), P())
    return jax.shard_map(
        local,
        mesh=mesh,
        in_specs=placed,
        out_specs=(P("ctx", "ch"), P("ctx", "ch"), P("ctx", "ch"), P(), P(), P()),
        check_vma=False,
    )
```

```python
import functools
import math

import jax
import jax.numpy as jnp
from jax import lax
from jax.experimental import pallas as pl
from jax.experimental.pallas import tpu as pltpu
from jax.sharding import PartitionSpec as P

GROUP = 16
POLES = 16
OWN = 8
BLK = 256
TOK = 128

MESH = pl.DeviceIdType.MESH
F32 = jnp.float32
BF16 = jnp.bfloat16
HIGHEST = lax.Precision.HIGHEST


def iota(shape, dim):
    return lax.broadcasted_iota(jnp.int32, shape, dim)


def dot(a, b, dims=((1,), (0,)), precision=None):
    return lax.dot_general(
        a, b, (dims, ((), ())), precision=precision, preferred_element_type=F32
    )


def comm_kernel(
    nsb, nch,
    q_hbm, k_hbm, v_hbm, c_hbm, res_hbm, log_hbm, skip_hbm,
    gq_ref, gk_ref, gv_ref, gr_ref, gl_ref, gs_ref,
    q_ref, k_ref, v_ref, c_ref, in_sem, log_ref, res_ref, skip_ref, par_sem, lam_s, res_s,
    x_s, d_s, ed_s, el_s, ed2_s, el2_s, h_s, hr_s, zl_s, fl_s,
    p1s, p1r, pms, pmr, p2s, p2r, p3s, p3r, pbs, pbr, p4s, p4r, p5s, p5r, coef_s, place_s, swap_s, swap_r, sh,
    s1, r1, sm, rm, s2, r2, s3, r3, sb_, rb_, s4, r4, s5, r5,
):
    ctx = lax.axis_index("ctx")
    ch = lax.axis_index("ch")
    own = ctx % OWN
    sup = ctx // OWN

    def load(i, n):
        cols = pl.ds(pl.multiple_of(i * BLK, BLK), BLK)
        src, dst = ((q_hbm, q_ref), (k_hbm, k_ref), (v_hbm, v_ref), (c_hbm, c_ref))[n]
        return pltpu.make_async_copy(src.at[:, cols], dst.at[:, cols], in_sem.at[i, n])

    shard = pl.ds(pl.multiple_of(ch * TOK, TOK), TOK)
    wide_shard = pl.ds(pl.multiple_of(ch * (OWN * BLK), OWN * BLK), OWN * BLK)
    params = [
        pltpu.make_async_copy(log_hbm.at[:, shard], log_ref, par_sem.at[0]),
        pltpu.make_async_copy(res_hbm.at[:, shard], res_ref, par_sem.at[1]),
        pltpu.make_async_copy(skip_hbm.at[:, wide_shard], skip_ref, par_sem.at[2]),
    ]
    for copy in params:
        copy.start()

    @pl.loop(0, OWN)
    def _(i):
        for n in range(4):
            load(i, n).start()

    barrier = pltpu.get_barrier_semaphore()

    def greet(ctx_to, ch_to):
        pl.semaphore_signal(barrier, inc=1, device_id=(ctx_to, ch_to), device_id_type=MESH)

    @pl.loop(1, OWN)
    def _(j):
        greet(sup * OWN + (own + j) % OWN, ch)

    @pl.loop(1, nsb)
    def _(j):
        greet(((sup + j) % nsb) * OWN + own, ch)

    @pl.loop(1, nch)
    def _(i):
        @pl.loop(0, OWN)
        def _(j):
            greet(sup * OWN + j, (ch + i) % nch)

    lane_t = iota((GROUP, TOK), 1).astype(F32)
    same_group = (iota((BLK, BLK), 0) % 16) == (iota((BLK, BLK), 1) // 16)
    pick_pole = ((iota((POLES, BLK), 1) // 16) == iota((POLES, BLK), 0)).astype(BF16)
    spread_pole = ((iota((BLK, POLES), 0) // 16) == iota((BLK, POLES), 1)).astype(BF16)

    for copy in params:
        copy.wait()
    lam_s[...] = jnp.exp(log_ref[...]).T
    res_s[...] = res_ref[...].T

    @pl.loop(0, OWN)
    def _(i):
        rows = pl.ds(pl.multiple_of(i * 16, 16), 16)
        lam = lam_s[rows, :]
        for p in range(POLES):
            lam_p = lam[:, p : p + 1]
            at = pl.ds(p * 16, 16)
            ed_s[i, at, :] = jnp.exp(-lam_p * lane_t).astype(BF16)
            el_s[i, at, :] = jnp.exp(-lam_p * (TOK - 1.0 - lane_t)).astype(BF16)

    @pl.loop(0, OWN)
    def _(i):
        cols = pl.ds(pl.multiple_of(i * BLK, BLK), BLK)
        for n in range(4):
            load(i, n).wait()
        x = (k_ref[:, cols].astype(F32) * v_ref[:, cols].astype(F32)).astype(BF16)
        d = (c_ref[:, cols].astype(F32) * q_ref[:, cols].astype(F32)).astype(BF16)
        x_s[:, cols] = x
        d_s[:, cols] = d
        for n, (table, val) in enumerate(((el_s, x), (ed_s, d))):
            full = jnp.where(same_group, dot(table[i], val), 0.0).astype(BF16)
            p1s[i, n] = dot(pick_pole, full).astype(BF16)

    pl.semaphore_wait(barrier, (OWN - 1) + (nsb - 1) + (nch - 1) * OWN)

    def to_own(j, src, dst, send, recv):
        other = (own + j) % OWN
        return pltpu.make_async_remote_copy(
            src_ref=src.at[other], dst_ref=dst.at[own], send_sem=send.at[other], recv_sem=recv.at[own],
            device_id=(sup * OWN + other, ch), device_id_type=MESH,
        )

    def from_own(j, src, dst, send, recv):
        other = (own + j) % OWN
        return pltpu.make_async_remote_copy(
            src_ref=src.at[other], dst_ref=dst.at[other], send_sem=send.at[other], recv_sem=recv.at[other],
            device_id=(sup * OWN + other, ch), device_id_type=MESH,
        )

    def send_own(*args):
        @pl.loop(1, OWN)
        def _(j):
            to_own(j, *args).start()

    def wait_own(*args):
        @pl.loop(1, OWN)
        def _(j):
            from_own(j, *args).wait_recv()

    def sent_own(*args):
        @pl.loop(1, OWN)
        def _(j):
            from_own(j, *args).wait_send()

    send_own(p1s, p1r, s1, r1)
    p1r[own] = p1s[own]

    @pl.loop(0, OWN)
    def _(i):
        rows = pl.ds(pl.multiple_of(i * 16, 16), 16)
        cols = pl.ds(pl.multiple_of(i * BLK, BLK), BLK)
        lam = lam_s[rows, :]
        res = res_s[rows, :]
        taps = jnp.zeros((GROUP, TOK), F32)
        back = jnp.zeros((GROUP, TOK), F32)
        for p in range(POLES):
            lam_p = lam[:, p : p + 1]
            res_p = res[:, p : p + 1]
            ed = jnp.exp(-lam_p * lane_t)
            el = jnp.exp(-lam_p * (TOK - 1.0 - lane_t))
            at = pl.ds(p * 16, 16)
            ed2_s[i, at, :] = (ed * (lane_t + 1.0)).astype(BF16)
            el2_s[i, at, :] = (el * (TOK - 1.0 - lane_t)).astype(BF16)
            taps = taps + res_p * ed
            back = back + (res_p * jnp.exp(-lam_p)) * el
        h_s[i] = taps
        hr_s[i] = jnp.where(lane_t == 0.0, taps, back)
        x = x_s[:, cols]
        d = d_s[:, cols]
        pbs[i, 2:3, :] = jnp.sum(x.astype(F32) * d.astype(F32), axis=0, keepdims=True)
        for n, (table, val) in enumerate(((el2_s, x), (ed2_s, d))):
            full = jnp.where(same_group, dot(table[i], val), 0.0).astype(BF16)
            pms[i, n] = dot(pick_pole, full).astype(BF16)

    send_own(pms, pmr, sm, rm)
    pmr[own] = pms[own]

    row_t = iota((TOK, TOK), 0)
    col_t = iota((TOK, TOK), 1)
    lane_group = iota((TOK, BLK), 1) // 16

    lane_row = iota((16, BLK), 1)
    diag = (lane_row % 16) == iota((16, BLK), 0)
    flip = (row_t == TOK - 1 - col_t).astype(BF16)

    rows = pl.ds(pl.multiple_of(own * 16, 16), 16)
    lam_own = lam_s[rows, :]
    res_own = res_s[rows, :]
    to_chan = ((iota((16, BLK), 1) // 16) == iota((16, BLK), 0)).astype(F32)
    lam_pc = dot(lam_own, to_chan, ((0,), (0,)), HIGHEST)
    res_pc = dot(res_own, to_chan, ((0,), (0,)), HIGHEST)
    w = jnp.exp(-float(TOK) * lam_pc)
    e1 = jnp.exp(-lam_pc)
    re1 = res_pc * e1

    wait_own(p1s, p1r, s1, r1)
    sum_l = jnp.zeros((POLES, BLK), F32)
    sum_d = jnp.zeros((POLES, BLK), F32)
    for b in range(OWN):
        sum_l = w * sum_l + p1r[b, 0].astype(F32)
        sum_d = w * sum_d + p1r[OWN - 1 - b, 1].astype(F32)
    p2s[0] = sum_l.astype(BF16)
    p2s[1] = sum_d.astype(BF16)

    col = sup // 2
    half = sup % 2
    ncol = nsb // 2

    def col_copy(j, slot):
        other = (col + j) % ncol
        later = (other > col).astype(jnp.int32)
        return pltpu.make_async_remote_copy(
            src_ref=p2s.at[1 - later], dst_ref=p2r.at[slot], send_sem=s2.at[other], recv_sem=r2.at[slot],
            device_id=((other * 2 + half) * OWN + own, ch), device_id_type=MESH,
        )

    def half_copy():
        return pltpu.make_async_remote_copy(
            src_ref=swap_s, dst_ref=swap_r, send_sem=sh.at[0], recv_sem=sh.at[1],
            device_id=((col * 2 + 1 - half) * OWN + own, ch), device_id_type=MESH,
        )

    @pl.loop(1, ncol)
    def _(j):
        col_copy(j, col).start()

    scale = dot(
        -lam_own * res_own, ((iota((POLES, BLK), 1) // 16) == iota((POLES, BLK), 0)).astype(F32), precision=HIGHEST
    )
    scale_row = jnp.sum(jnp.where(diag, scale, 0.0), axis=0, keepdims=True)

    @pl.loop(0, ncol)
    def _(b):
        gap = jnp.maximum(jnp.abs(col - b) - 1, 0).astype(F32) * float(TOK * OWN * 2)
        coef_s[b] = jnp.exp(-lam_pc * gap)

    wide_w = jnp.exp(-float(TOK * OWN) * lam_pc)
    wide_w2 = jnp.exp(-float(TOK * OWN * 2) * lam_pc)

    place_s[...] = (
        (iota((OWN * BLK, TOK), 0) // BLK == iota((OWN * BLK, TOK), 1) // 16)
        & (iota((OWN * BLK, TOK), 0) % 16 == iota((OWN * BLK, TOK), 1) % 16)
    ).astype(BF16)
    zero = jnp.zeros((POLES, BLK), F32)

    def gather(j, sums):
        other = (col + j) % ncol
        col_copy(j, other).wait_recv()
        term = coef_s[other] * p2r[other].astype(F32)
        later = other > col
        return sums[0] + jnp.where(later, 0.0, term), sums[1] + jnp.where(later, term, 0.0)

    col_s, col_f = lax.fori_loop(1, ncol, gather, (zero, zero))
    swap_s[0] = jnp.where(half == 0, sum_l + wide_w2 * col_s, col_s).astype(BF16)
    swap_s[1] = jnp.where(half == 0, col_f, sum_d + wide_w2 * col_f).astype(BF16)
    half_copy().start()

    @pl.loop(0, OWN)
    def _(i):
        cols = pl.ds(pl.multiple_of(i * BLK, BLK), BLK)
        x = dot(flip, x_s[:, cols]).astype(BF16)
        d = d_s[:, cols]
        sums = []
        for g in range(16):
            dm = jnp.where(lane_group == g, d, jnp.zeros_like(d))
            corr = dot(x, dm, ((1,), (1,)))
            corr = jnp.where(col_t >= TOK - 1 - row_t, corr, 0.0)
            corr = pltpu.roll(corr, 1, 1, stride=1, stride_axis=0)
            sums.append(jnp.sum(corr, axis=0, keepdims=True))
        fg = jnp.concatenate(sums, axis=0)
        hi = fg.astype(BF16)
        lo = (fg - hi.astype(F32)).astype(BF16)
        both = jnp.concatenate([hi, lo], axis=0)
        r_in = dot(both, ed_s[i], ((1,), (1,)))
        m_in = dot(both, ed2_s[i], ((1,), (1,)))
        r_in = r_in[:16] + r_in[16:]
        m_in = m_in[:16] + m_in[16:] - r_in
        pbs[i, 0:1, :] = jnp.sum(jnp.where(diag, r_in, 0.0), axis=0, keepdims=True)
        pbs[i, 1:2, :] = jnp.sum(jnp.where(diag, m_in, 0.0), axis=0, keepdims=True)
        pbs[i, 3:4, :] = jnp.zeros((1, BLK), F32)

    send_own(pbs, pbr, sb_, rb_)
    pbr[own] = pbs[own]

    @pl.loop(0, OWN)
    def _(i):
        cols = pl.ds(pl.multiple_of(i * BLK, BLK), BLK)
        x = x_s[:, cols]
        acc = jnp.zeros((TOK, BLK), F32)
        hr = hr_s[i]
        for g in range(16):
            wide = jnp.broadcast_to(hr[g : g + 1, :], (TOK, TOK))
            mat = pltpu.roll(wide, 0, 1, stride=1, stride_axis=0)
            mat = jnp.where(col_t <= row_t, mat, 0.0).astype(BF16)
            acc = jnp.where(lane_group == g, dot(mat, x), acc)
        zl_s[:, cols] = acc

    wait_own(pms, pmr, sm, rm)
    wait_own(pbs, pbr, sb_, rb_)
    part = pbr[0]
    for b in range(1, OWN):
        part = part + pbr[b]

    half_copy().wait_recv()
    in_s = wide_w * col_s + swap_r[0].astype(F32)
    in_f = wide_w * col_f + swap_r[1].astype(F32)
    carry_s = []
    for b in range(OWN):
        carry_s.append(in_s)
        p3s[b, 0] = (re1 * in_s).astype(BF16)
        in_s = w * in_s + p1r[b, 0].astype(F32)
    r_sum = jnp.zeros((POLES, BLK), F32)
    m_sum = jnp.zeros((POLES, BLK), F32)
    for b in reversed(range(OWN)):
        p3s[b, 1] = (re1 * in_f).astype(BF16)
        d_b = p1r[b, 1].astype(F32)
        r_sum = r_sum + d_b * carry_s[b]
        m_sum = (
            m_sum
            + pmr[b, 1].astype(F32) * carry_s[b]
            + pmr[b, 0].astype(F32) * in_f
            + (float(TOK) * w) * (carry_s[b] * in_f)
        )
        in_f = w * in_f + d_b
    def pack(first, second, third):
        half = BLK // 2
        top = jnp.concatenate([first, second[:, :half]], axis=1)
        low = jnp.concatenate([second[:, half:], third], axis=1)
        return jnp.concatenate([top, low], axis=0).astype(BF16)

    def unpack(val):
        half = BLK // 2
        second = jnp.concatenate([val[0:1, BLK:], val[1:2, :half]], axis=1)
        return val[0:1, :BLK], second, val[1:2, half:]

    chan_group = ((iota((BLK, BLK), 0) // 16) == (iota((BLK, BLK), 1) % 16)).astype(F32)
    pole_row = (iota((POLES, BLK), 1) // 16) == iota((POLES, BLK), 0)
    sums = dot(jnp.concatenate([r_sum * e1, m_sum * e1], axis=0), chan_group, precision=HIGHEST)
    r_row = jnp.sum(jnp.where(pole_row, sums[:POLES], 0.0), axis=0, keepdims=True)
    m_row = jnp.sum(jnp.where(pole_row, sums[POLES:], 0.0), axis=0, keepdims=True)
    p4s[...] = pack(part[0:1] + r_row, part[1:2] + m_row, part[2:3])

    def grad_copy(j, slot):
        other = (sup + j) % nsb
        return pltpu.make_async_remote_copy(
            src_ref=p4s, dst_ref=p4r.at[slot], send_sem=s4.at[other], recv_sem=r4.at[slot],
            device_id=(other * OWN + own, ch), device_id_type=MESH,
        )

    @pl.loop(1, nsb)
    def _(j):
        grad_copy(j, sup).start()

    send_own(p3s, p3r, s3, r3)
    p3r[own] = p3s[own]
    p4r[sup] = p4s[...]

    @pl.loop(0, OWN)
    def _(i):
        cols = pl.ds(pl.multiple_of(i * BLK, BLK), BLK)
        d = d_s[:, cols]
        acc = jnp.zeros((TOK, BLK), F32)
        h = h_s[i]
        for g in range(16):
            wide = jnp.broadcast_to(h[g : g + 1, :], (TOK, TOK))
            mat = pltpu.roll(wide, 0, 1, stride=1, stride_axis=0)
            mat = jnp.where(col_t >= row_t, mat, 0.0).astype(BF16)
            acc = jnp.where(lane_group == g, dot(mat, d), acc)
        fl_s[:, cols] = acc

    @pl.loop(0, OWN)
    def _(j):
        i = (own + j) % OWN

        @pl.when(j > 0)
        def _():
            from_own(j, p3s, p3r, s3, r3).wait_recv()

        cols = pl.ds(pl.multiple_of(i * BLK, BLK), BLK)
        skip = skip_ref[:, cols]
        both = []
        for n, (table, src, loc) in enumerate(((ed_s, x_s, zl_s), (el_s, d_s, fl_s))):
            wide = dot(spread_pole, p3r[i, n])
            wide = jnp.where(same_group, wide, 0.0).astype(BF16)
            corr = dot(table[i], wide, ((0,), (0,)))
            out = skip * src[:, cols].astype(F32) + (loc[:, cols] + corr)
            both.append(out.astype(BF16).astype(F32))
        hidden, flow = both
        gq_ref[:, cols] = (c_ref[:, cols].astype(F32) * hidden).astype(BF16)
        gk_ref[:, cols] = (flow * v_ref[:, cols].astype(F32)).astype(BF16)
        gv_ref[:, cols] = (flow * k_ref[:, cols].astype(F32)).astype(BF16)

    length = float(TOK * OWN * nsb)

    @pl.loop(1, nsb)
    def _(j):
        grad_copy(j, (sup + j) % nsb).wait_recv()

    total = p4r[0].astype(F32)
    for b in range(1, nsb):
        total = total + p4r[b].astype(F32)
    r_row, m_row, k_row = unpack(total)
    p5s[...] = pack(r_row / length, m_row * scale_row / math.sqrt(length), k_row / math.sqrt(length))

    def last_copy(i, j, mine):
        ch_to = (ch + i) % nch
        own_to = (own + j) % OWN
        here = ch * OWN + own
        there = ch_to * OWN + own_to
        slot = here if mine else there
        return pltpu.make_async_remote_copy(
            src_ref=p5s, dst_ref=p5r.at[slot], send_sem=s5.at[there], recv_sem=r5.at[slot],
            device_id=(sup * OWN + own_to, ch_to), device_id_type=MESH,
        )

    @pl.loop(1, nch * OWN)
    def _(n):
        last_copy(n // OWN, n % OWN, True).start()

    p5r[ch * OWN + own] = p5s[...]

    sent_own(p1s, p1r, s1, r1)
    sent_own(pms, pmr, sm, rm)
    sent_own(pbs, pbr, sb_, rb_)
    sent_own(p3s, p3r, s3, r3)

    half_copy().wait_send()

    @pl.loop(1, ncol)
    def _(j):
        col_copy(j, col).wait_send()

    @pl.loop(1, nsb)
    def _(j):
        grad_copy(j, sup).wait_send()

    @pl.loop(1, nch * OWN)
    def _(n):
        last_copy(n // OWN, n % OWN, False).wait_recv()

    @pl.loop(1, nch * OWN)
    def _(n):
        last_copy(n // OWN, n % OWN, True).wait_send()

    keep = (iota((POLES, OWN * BLK), 1) % BLK) // 16 == iota((POLES, OWN * BLK), 0)
    for i in range(nch):
        rows = [unpack(p5r[i * OWN + j].astype(F32)) for j in range(OWN)]
        parts = []
        for n in range(2):
            row = jnp.concatenate([val[n] for val in rows], axis=1)
            parts.append(jnp.where(keep, jnp.broadcast_to(row, keep.shape), 0.0).astype(BF16))
        got = dot(jnp.concatenate(parts, axis=0), place_s[...])
        gr_ref[:, i * TOK : (i + 1) * TOK] = got[:POLES]
        gl_ref[:, i * TOK : (i + 1) * TOK] = got[POLES:]
        for j in range(OWN):
            n = i * OWN + j
            gs_ref[:, n * BLK : (n + 1) * BLK] = rows[j][2]


def exchange(queries, key_input, value_input, cotangent, residues, log_rates, skip_row):
    nsb = lax.axis_size("ctx") // OWN
    nch = lax.axis_size("ch")
    width = OWN * BLK
    vmem = pl.BlockSpec(memory_space=pltpu.VMEM)
    dma = pltpu.SemaphoreType.DMA
    state = (POLES, BLK)
    return pl.pallas_call(
        functools.partial(comm_kernel, nsb, nch),
        out_shape=(
            *[jax.ShapeDtypeStruct((TOK, width), BF16)] * 3,
            *[jax.ShapeDtypeStruct((POLES, nch * TOK), F32)] * 2,
            jax.ShapeDtypeStruct((1, nch * width), F32),
        ),
        in_specs=[pl.BlockSpec(memory_space=pltpu.HBM)] * 7,
        out_specs=(vmem,) * 6,
        scratch_shapes=[
            *[pltpu.VMEM((TOK, width), BF16)] * 4,
            dma((OWN, 4)),
            pltpu.VMEM((POLES, TOK), F32),
            pltpu.VMEM((POLES, TOK), F32),
            pltpu.VMEM((1, width), F32),
            dma((3,)),
            pltpu.VMEM((TOK, POLES), F32),
            pltpu.VMEM((TOK, POLES), F32),
            pltpu.VMEM((TOK, width), BF16),
            pltpu.VMEM((TOK, width), BF16),
            *[pltpu.VMEM((OWN, BLK, TOK), BF16)] * 4,
            pltpu.VMEM((OWN, GROUP, TOK), F32),
            pltpu.VMEM((OWN, GROUP, TOK), F32),
            pltpu.VMEM((TOK, width), F32),
            pltpu.VMEM((TOK, width), F32),
            *[pltpu.VMEM((OWN, 2) + state, BF16)] * 4,
            pltpu.VMEM((2,) + state, BF16),
            pltpu.VMEM((nsb // 2,) + state, BF16),
            pltpu.VMEM((OWN, 2) + state, BF16),
            pltpu.VMEM((OWN, 2) + state, BF16),
            pltpu.VMEM((OWN, 4, BLK), F32),
            pltpu.VMEM((OWN, 4, BLK), F32),
            pltpu.VMEM((2, 3 * BLK // 2), BF16),
            pltpu.VMEM((nsb, 2, 3 * BLK // 2), BF16),
            pltpu.VMEM((2, 3 * BLK // 2), BF16),
            pltpu.VMEM((nch * OWN, 2, 3 * BLK // 2), BF16),
            pltpu.VMEM((nsb // 2,) + state, F32),
            pltpu.VMEM((OWN * BLK, TOK), BF16),
            pltpu.VMEM((2,) + state, BF16),
            pltpu.VMEM((2,) + state, BF16),
            dma((2,)),
            dma((OWN,)), dma((OWN,)),
            dma((OWN,)), dma((OWN,)),
            dma((nsb // 2,)), dma((nsb // 2,)),
            dma((OWN,)), dma((OWN,)),
            dma((OWN,)), dma((OWN,)),
            dma((nsb,)), dma((nsb,)),
            dma((nch * OWN,)), dma((nch * OWN,)),
        ],
        compiler_params=pltpu.CompilerParams(
            collective_id=0, has_side_effects=True, vmem_limit_bytes=48 << 20
        ),
        name="exchange",
    )(
        *[
            pltpu.with_memory_space_constraint(val, pltpu.HBM)
            for val in (queries, key_input, value_input, cotangent, residues, log_rates, skip_row)
        ]
    )


def store_kernel(*refs):
    count = (len(refs) - 1) // 2
    sem = refs[-1]
    copies = [pltpu.make_async_copy(refs[n], refs[count + n], sem.at[n]) for n in range(count)]
    for copy in copies:
        copy.start()
    for copy in copies:
        copy.wait()


def store(*arrays):
    count = len(arrays)
    return pl.pallas_call(
        store_kernel,
        out_shape=tuple(jax.ShapeDtypeStruct(val.shape, val.dtype) for val in arrays),
        in_specs=[pl.BlockSpec(memory_space=pltpu.VMEM)] * count,
        out_specs=(pl.BlockSpec(memory_space=pltpu.HBM),) * count,
        scratch_shapes=[pltpu.SemaphoreType.DMA((count,))],
        compiler_params=pltpu.CompilerParams(vmem_limit_bytes=1 << 20),
        name="store",
    )(*arrays)


def local(queries, key_input, value_input, cotangent, residues, log_rates, skip_gain):
    gq, gk, gv, gr, gl, gs = store(*exchange(
        queries, key_input, value_input, cotangent, residues.T, log_rates.T, skip_gain.reshape(1, -1)
    ))
    return (gq, gk, gv, gr.T, gl.T, gs.reshape(-1))


def solution(mesh):
    placed = (P("ctx", "ch"), P("ctx", "ch"), P("ctx", "ch"), P("ctx", "ch"), P(), P(), P())
    return jax.shard_map(
        local,
        mesh=mesh,
        in_specs=placed,
        out_specs=(P("ctx", "ch"), P("ctx", "ch"), P("ctx", "ch"), P(), P(), P()),
        check_vma=False,
    )
```

```python
import functools
import math

import jax
import jax.numpy as jnp
from jax import lax
from jax.experimental import pallas as pl
from jax.experimental.pallas import tpu as pltpu
from jax.sharding import PartitionSpec as P

GROUP = 16
POLES = 16
OWN = 8
BLK = 256
TOK = 128

MESH = pl.DeviceIdType.MESH
F32 = jnp.float32
BF16 = jnp.bfloat16
HIGHEST = lax.Precision.HIGHEST


def iota(shape, dim):
    return lax.broadcasted_iota(jnp.int32, shape, dim)


def dot(a, b, dims=((1,), (0,)), precision=None):
    return lax.dot_general(
        a, b, (dims, ((), ())), precision=precision, preferred_element_type=F32
    )


def comm_kernel(
    nsb, nch,
    q_hbm, k_hbm, v_hbm, c_hbm, res_hbm, log_hbm, skip_hbm,
    gq_ref, gk_ref, gv_ref, gr_ref, gl_ref, gs_ref,
    q_ref, k_ref, v_ref, c_ref, in_sem, log_ref, res_ref, skip_ref, par_sem, lam_s, res_s,
    x_s, d_s, ed_s, el_s, ed2_s, el2_s, h_s, hr_s, zl_s, fl_s,
    p1s, p1r, pms, pmr, p2s, p2r, p3s, p3r, pbs, pbr, p4s, p4r, p5s, p5r, coef_s, place_s, swap_s, swap_r, sh,
    s1, r1, sm, rm, s2, r2, s3, r3, sb_, rb_, s4, r4, s5, r5,
):
    ctx = lax.axis_index("ctx")
    ch = lax.axis_index("ch")
    own = ctx % OWN
    sup = ctx // OWN
    col = sup // 2
    half = sup % 2
    ncol = nsb // 2
    plane = 2 * nch * OWN
    here = (half * nch + ch) * OWN + own

    def load(i, n):
        cols = pl.ds(pl.multiple_of(i * BLK, BLK), BLK)
        src, dst = ((q_hbm, q_ref), (k_hbm, k_ref), (v_hbm, v_ref), (c_hbm, c_ref))[n]
        return pltpu.make_async_copy(src.at[:, cols], dst.at[:, cols], in_sem.at[i, n])

    shard = pl.ds(pl.multiple_of(ch * TOK, TOK), TOK)
    wide_shard = pl.ds(pl.multiple_of(ch * (OWN * BLK), OWN * BLK), OWN * BLK)
    params = [
        pltpu.make_async_copy(log_hbm.at[:, shard], log_ref, par_sem.at[0]),
        pltpu.make_async_copy(res_hbm.at[:, shard], res_ref, par_sem.at[1]),
        pltpu.make_async_copy(skip_hbm.at[:, wide_shard], skip_ref, par_sem.at[2]),
    ]
    for copy in params:
        copy.start()

    @pl.loop(0, OWN)
    def _(i):
        for n in range(4):
            load(i, n).start()

    barrier = pltpu.get_barrier_semaphore()

    def greet(ctx_to, ch_to):
        pl.semaphore_signal(barrier, inc=1, device_id=(ctx_to, ch_to), device_id_type=MESH)

    @pl.loop(1, plane)
    def _(n):
        there = (here + n) % plane
        greet((col * 2 + there // (nch * OWN)) * OWN + there % OWN, (there // OWN) % nch)

    @pl.loop(1, ncol)
    def _(j):
        greet((((col + j) % ncol) * 2 + half) * OWN + own, ch)

    lane_t = iota((GROUP, TOK), 1).astype(F32)
    same_group = (iota((BLK, BLK), 0) % 16) == (iota((BLK, BLK), 1) // 16)
    pick_pole = ((iota((POLES, BLK), 1) // 16) == iota((POLES, BLK), 0)).astype(BF16)
    spread_pole = ((iota((BLK, POLES), 0) // 16) == iota((BLK, POLES), 1)).astype(BF16)

    for copy in params:
        copy.wait()
    lam_s[...] = jnp.exp(log_ref[...]).T
    res_s[...] = res_ref[...].T

    @pl.loop(0, OWN)
    def _(i):
        rows = pl.ds(pl.multiple_of(i * 16, 16), 16)
        lam = lam_s[rows, :]
        for p in range(POLES):
            lam_p = lam[:, p : p + 1]
            at = pl.ds(p * 16, 16)
            ed_s[i, at, :] = jnp.exp(-lam_p * lane_t).astype(BF16)
            el_s[i, at, :] = jnp.exp(-lam_p * (TOK - 1.0 - lane_t)).astype(BF16)

    @pl.loop(0, OWN)
    def _(i):
        cols = pl.ds(pl.multiple_of(i * BLK, BLK), BLK)
        for n in range(4):
            load(i, n).wait()
        x = (k_ref[:, cols].astype(F32) * v_ref[:, cols].astype(F32)).astype(BF16)
        d = (c_ref[:, cols].astype(F32) * q_ref[:, cols].astype(F32)).astype(BF16)
        x_s[:, cols] = x
        d_s[:, cols] = d
        for n, (table, val) in enumerate(((el_s, x), (ed_s, d))):
            full = jnp.where(same_group, dot(table[i], val), 0.0).astype(BF16)
            p1s[i, n] = dot(pick_pole, full).astype(BF16)

    pl.semaphore_wait(barrier, (plane - 1) + (ncol - 1))

    def to_own(j, src, dst, send, recv):
        other = (own + j) % OWN
        return pltpu.make_async_remote_copy(
            src_ref=src.at[other], dst_ref=dst.at[own], send_sem=send.at[other], recv_sem=recv.at[own],
            device_id=(sup * OWN + other, ch), device_id_type=MESH,
        )

    def from_own(j, src, dst, send, recv):
        other = (own + j) % OWN
        return pltpu.make_async_remote_copy(
            src_ref=src.at[other], dst_ref=dst.at[other], send_sem=send.at[other], recv_sem=recv.at[other],
            device_id=(sup * OWN + other, ch), device_id_type=MESH,
        )

    def send_own(*args):
        @pl.loop(1, OWN)
        def _(j):
            to_own(j, *args).start()

    def wait_own(*args):
        @pl.loop(1, OWN)
        def _(j):
            from_own(j, *args).wait_recv()

    def sent_own(*args):
        @pl.loop(1, OWN)
        def _(j):
            from_own(j, *args).wait_send()

    send_own(p1s, p1r, s1, r1)
    p1r[own] = p1s[own]

    @pl.loop(0, OWN)
    def _(i):
        rows = pl.ds(pl.multiple_of(i * 16, 16), 16)
        cols = pl.ds(pl.multiple_of(i * BLK, BLK), BLK)
        lam = lam_s[rows, :]
        res = res_s[rows, :]
        taps = jnp.zeros((GROUP, TOK), F32)
        back = jnp.zeros((GROUP, TOK), F32)
        for p in range(POLES):
            lam_p = lam[:, p : p + 1]
            res_p = res[:, p : p + 1]
            ed = jnp.exp(-lam_p * lane_t)
            el = jnp.exp(-lam_p * (TOK - 1.0 - lane_t))
            at = pl.ds(p * 16, 16)
            ed2_s[i, at, :] = (ed * (lane_t + 1.0)).astype(BF16)
            el2_s[i, at, :] = (el * (TOK - 1.0 - lane_t)).astype(BF16)
            taps = taps + res_p * ed
            back = back + (res_p * jnp.exp(-lam_p)) * el
        h_s[i] = taps
        hr_s[i] = jnp.where(lane_t == 0.0, taps, back)
        x = x_s[:, cols]
        d = d_s[:, cols]
        pbs[i, 2:3, :] = jnp.sum(x.astype(F32) * d.astype(F32), axis=0, keepdims=True)
        for n, (table, val) in enumerate(((el2_s, x), (ed2_s, d))):
            full = jnp.where(same_group, dot(table[i], val), 0.0).astype(BF16)
            pms[i, n] = dot(pick_pole, full).astype(BF16)

    send_own(pms, pmr, sm, rm)
    pmr[own] = pms[own]

    row_t = iota((TOK, TOK), 0)
    col_t = iota((TOK, TOK), 1)
    lane_group = iota((TOK, BLK), 1) // 16

    lane_row = iota((16, BLK), 1)
    diag = (lane_row % 16) == iota((16, BLK), 0)
    flip = (row_t == TOK - 1 - col_t).astype(BF16)

    @pl.loop(0, OWN)
    def _(i):
        cols = pl.ds(pl.multiple_of(i * BLK, BLK), BLK)
        x = x_s[:, cols]
        acc = jnp.zeros((TOK, BLK), F32)
        hr = hr_s[i]
        for g in range(16):
            wide = jnp.broadcast_to(hr[g : g + 1, :], (TOK, TOK))
            mat = pltpu.roll(wide, 0, 1, stride=1, stride_axis=0)
            mat = jnp.where(col_t <= row_t, mat, 0.0).astype(BF16)
            acc = jnp.where(lane_group == g, dot(mat, x), acc)
        zl_s[:, cols] = acc

    rows = pl.ds(pl.multiple_of(own * 16, 16), 16)
    lam_own = lam_s[rows, :]
    res_own = res_s[rows, :]
    to_chan = ((iota((16, BLK), 1) // 16) == iota((16, BLK), 0)).astype(F32)
    lam_pc = dot(lam_own, to_chan, ((0,), (0,)), HIGHEST)
    res_pc = dot(res_own, to_chan, ((0,), (0,)), HIGHEST)
    w = jnp.exp(-float(TOK) * lam_pc)
    e1 = jnp.exp(-lam_pc)
    re1 = res_pc * e1

    wait_own(p1s, p1r, s1, r1)
    sum_l = jnp.zeros((POLES, BLK), F32)
    sum_d = jnp.zeros((POLES, BLK), F32)
    for b in range(OWN):
        sum_l = w * sum_l + p1r[b, 0].astype(F32)
        sum_d = w * sum_d + p1r[OWN - 1 - b, 1].astype(F32)
    p2s[0] = sum_l.astype(BF16)
    p2s[1] = sum_d.astype(BF16)


    def col_copy(j, slot):
        other = (col + j) % ncol
        later = (other > col).astype(jnp.int32)
        return pltpu.make_async_remote_copy(
            src_ref=p2s.at[1 - later], dst_ref=p2r.at[slot], send_sem=s2.at[other], recv_sem=r2.at[slot],
            device_id=((other * 2 + half) * OWN + own, ch), device_id_type=MESH,
        )

    def half_copy():
        return pltpu.make_async_remote_copy(
            src_ref=swap_s, dst_ref=swap_r, send_sem=sh.at[0], recv_sem=sh.at[1],
            device_id=((col * 2 + 1 - half) * OWN + own, ch), device_id_type=MESH,
        )

    @pl.loop(1, ncol)
    def _(j):
        col_copy(j, col).start()

    scale = dot(
        -lam_own * res_own, ((iota((POLES, BLK), 1) // 16) == iota((POLES, BLK), 0)).astype(F32), precision=HIGHEST
    )
    scale_row = jnp.sum(jnp.where(diag, scale, 0.0), axis=0, keepdims=True)

    @pl.loop(0, ncol)
    def _(b):
        gap = jnp.maximum(jnp.abs(col - b) - 1, 0).astype(F32) * float(TOK * OWN * 2)
        coef_s[b] = jnp.exp(-lam_pc * gap)

    wide_w = jnp.exp(-float(TOK * OWN) * lam_pc)
    wide_w2 = jnp.exp(-float(TOK * OWN * 2) * lam_pc)

    place_s[...] = (
        (iota((OWN * BLK, TOK), 0) // BLK == iota((OWN * BLK, TOK), 1) // 16)
        & (iota((OWN * BLK, TOK), 0) % 16 == iota((OWN * BLK, TOK), 1) % 16)
    ).astype(BF16)
    zero = jnp.zeros((POLES, BLK), F32)

    def gather(j, sums):
        other = (col + j) % ncol
        col_copy(j, other).wait_recv()
        term = coef_s[other] * p2r[other].astype(F32)
        later = other > col
        return sums[0] + jnp.where(later, 0.0, term), sums[1] + jnp.where(later, term, 0.0)

    col_s, col_f = lax.fori_loop(1, ncol, gather, (zero, zero))
    swap_s[0] = jnp.where(half == 0, sum_l + wide_w2 * col_s, col_s).astype(BF16)
    swap_s[1] = jnp.where(half == 0, col_f, sum_d + wide_w2 * col_f).astype(BF16)
    half_copy().start()

    @pl.loop(0, OWN)
    def _(i):
        cols = pl.ds(pl.multiple_of(i * BLK, BLK), BLK)
        x = dot(flip, x_s[:, cols]).astype(BF16)
        d = d_s[:, cols]
        sums = []
        for g in range(16):
            dm = jnp.where(lane_group == g, d, jnp.zeros_like(d))
            corr = dot(x, dm, ((1,), (1,)))
            corr = jnp.where(col_t >= TOK - 1 - row_t, corr, 0.0)
            corr = pltpu.roll(corr, 1, 1, stride=1, stride_axis=0)
            sums.append(jnp.sum(corr, axis=0, keepdims=True))
        fg = jnp.concatenate(sums, axis=0)
        hi = fg.astype(BF16)
        lo = (fg - hi.astype(F32)).astype(BF16)
        both = jnp.concatenate([hi, lo], axis=0)
        r_in = dot(both, ed_s[i], ((1,), (1,)))
        m_in = dot(both, ed2_s[i], ((1,), (1,)))
        r_in = r_in[:16] + r_in[16:]
        m_in = m_in[:16] + m_in[16:] - r_in
        pbs[i, 0:1, :] = jnp.sum(jnp.where(diag, r_in, 0.0), axis=0, keepdims=True)
        pbs[i, 1:2, :] = jnp.sum(jnp.where(diag, m_in, 0.0), axis=0, keepdims=True)
        pbs[i, 3:4, :] = jnp.zeros((1, BLK), F32)

    send_own(pbs, pbr, sb_, rb_)
    pbr[own] = pbs[own]

    @pl.loop(0, OWN)
    def _(i):
        cols = pl.ds(pl.multiple_of(i * BLK, BLK), BLK)
        d = d_s[:, cols]
        acc = jnp.zeros((TOK, BLK), F32)
        h = h_s[i]
        for g in range(16):
            wide = jnp.broadcast_to(h[g : g + 1, :], (TOK, TOK))
            mat = pltpu.roll(wide, 0, 1, stride=1, stride_axis=0)
            mat = jnp.where(col_t >= row_t, mat, 0.0).astype(BF16)
            acc = jnp.where(lane_group == g, dot(mat, d), acc)
        fl_s[:, cols] = acc

    wait_own(pms, pmr, sm, rm)
    wait_own(pbs, pbr, sb_, rb_)
    part = pbr[0]
    for b in range(1, OWN):
        part = part + pbr[b]

    half_copy().wait_recv()
    in_s = wide_w * col_s + swap_r[0].astype(F32)
    in_f = wide_w * col_f + swap_r[1].astype(F32)
    carry_s = []
    for b in range(OWN):
        carry_s.append(in_s)
        p3s[b, 0] = (re1 * in_s).astype(BF16)
        in_s = w * in_s + p1r[b, 0].astype(F32)
    r_sum = jnp.zeros((POLES, BLK), F32)
    m_sum = jnp.zeros((POLES, BLK), F32)
    for b in reversed(range(OWN)):
        p3s[b, 1] = (re1 * in_f).astype(BF16)
        d_b = p1r[b, 1].astype(F32)
        r_sum = r_sum + d_b * carry_s[b]
        m_sum = (
            m_sum
            + pmr[b, 1].astype(F32) * carry_s[b]
            + pmr[b, 0].astype(F32) * in_f
            + (float(TOK) * w) * (carry_s[b] * in_f)
        )
        in_f = w * in_f + d_b
    def pack(first, second, third):
        half = BLK // 2
        top = jnp.concatenate([first, second[:, :half]], axis=1)
        low = jnp.concatenate([second[:, half:], third], axis=1)
        return jnp.concatenate([top, low], axis=0).astype(BF16)

    def unpack(val):
        half = BLK // 2
        second = jnp.concatenate([val[0:1, BLK:], val[1:2, :half]], axis=1)
        return val[0:1, :BLK], second, val[1:2, half:]

    chan_group = ((iota((BLK, BLK), 0) // 16) == (iota((BLK, BLK), 1) % 16)).astype(F32)
    pole_row = (iota((POLES, BLK), 1) // 16) == iota((POLES, BLK), 0)
    sums = dot(jnp.concatenate([r_sum * e1, m_sum * e1], axis=0), chan_group, precision=HIGHEST)
    r_row = jnp.sum(jnp.where(pole_row, sums[:POLES], 0.0), axis=0, keepdims=True)
    m_row = jnp.sum(jnp.where(pole_row, sums[POLES:], 0.0), axis=0, keepdims=True)
    p4s[...] = pack(part[0:1] + r_row, part[1:2] + m_row, part[2:3])

    def grad_copy(j, slot):
        other = (col + j) % ncol
        return pltpu.make_async_remote_copy(
            src_ref=p4s, dst_ref=p4r.at[slot], send_sem=s4.at[other], recv_sem=r4.at[slot],
            device_id=((other * 2 + half) * OWN + own, ch), device_id_type=MESH,
        )

    @pl.loop(1, ncol)
    def _(j):
        grad_copy(j, col).start()

    send_own(p3s, p3r, s3, r3)
    p3r[own] = p3s[own]
    p4r[col] = p4s[...]

    length = float(TOK * OWN * nsb)

    @pl.loop(1, ncol)
    def _(j):
        grad_copy(j, (col + j) % ncol).wait_recv()

    total = p4r[0].astype(F32)
    for b in range(1, ncol):
        total = total + p4r[b].astype(F32)
    r_row, m_row, k_row = unpack(total)
    p5s[...] = pack(r_row / length, m_row * scale_row / math.sqrt(length), k_row / math.sqrt(length))

    def last_copy(n, mine):
        there = (here + n) % plane
        slot = here if mine else there
        return pltpu.make_async_remote_copy(
            src_ref=p5s, dst_ref=p5r.at[slot], send_sem=s5.at[there], recv_sem=r5.at[slot],
            device_id=((col * 2 + there // (nch * OWN)) * OWN + there % OWN, (there // OWN) % nch),
            device_id_type=MESH,
        )

    for n in range(1, plane):
        last_copy(n, True).start()
    p5r[here] = p5s[...]

    @pl.loop(0, OWN)
    def _(j):
        i = (own + j) % OWN

        @pl.when(j > 0)
        def _():
            from_own(j, p3s, p3r, s3, r3).wait_recv()

        cols = pl.ds(pl.multiple_of(i * BLK, BLK), BLK)
        skip = skip_ref[:, cols]
        both = []
        for n, (table, src, loc) in enumerate(((ed_s, x_s, zl_s), (el_s, d_s, fl_s))):
            wide = dot(spread_pole, p3r[i, n])
            wide = jnp.where(same_group, wide, 0.0).astype(BF16)
            corr = dot(table[i], wide, ((0,), (0,)))
            out = skip * src[:, cols].astype(F32) + (loc[:, cols] + corr)
            both.append(out.astype(BF16).astype(F32))
        hidden, flow = both
        gq_ref[:, cols] = (c_ref[:, cols].astype(F32) * hidden).astype(BF16)
        gk_ref[:, cols] = (flow * v_ref[:, cols].astype(F32)).astype(BF16)
        gv_ref[:, cols] = (flow * k_ref[:, cols].astype(F32)).astype(BF16)

    sent_own(p1s, p1r, s1, r1)
    sent_own(pms, pmr, sm, rm)
    sent_own(pbs, pbr, sb_, rb_)
    sent_own(p3s, p3r, s3, r3)

    half_copy().wait_send()

    @pl.loop(1, ncol)
    def _(j):
        col_copy(j, col).wait_send()

    @pl.loop(1, ncol)
    def _(j):
        grad_copy(j, col).wait_send()

    @pl.loop(1, plane)
    def _(n):
        last_copy(n, True).wait_send()

    @pl.loop(1, plane)
    def _(n):
        last_copy(n, False).wait_recv()

    keep = (iota((POLES, OWN * BLK), 1) % BLK) // 16 == iota((POLES, OWN * BLK), 0)
    for i in range(nch):
        rows = [
            unpack(p5r[i * OWN + j].astype(F32) + p5r[(nch + i) * OWN + j].astype(F32)) for j in range(OWN)
        ]
        parts = []
        for n in range(2):
            row = jnp.concatenate([val[n] for val in rows], axis=1)
            parts.append(jnp.where(keep, jnp.broadcast_to(row, keep.shape), 0.0).astype(BF16))
        got = dot(jnp.concatenate(parts, axis=0), place_s[...])
        gr_ref[:, i * TOK : (i + 1) * TOK] = got[:POLES]
        gl_ref[:, i * TOK : (i + 1) * TOK] = got[POLES:]
        for j in range(OWN):
            n = i * OWN + j
            gs_ref[:, n * BLK : (n + 1) * BLK] = rows[j][2]


def exchange(queries, key_input, value_input, cotangent, residues, log_rates, skip_row):
    nsb = lax.axis_size("ctx") // OWN
    nch = lax.axis_size("ch")
    width = OWN * BLK
    vmem = pl.BlockSpec(memory_space=pltpu.VMEM)
    dma = pltpu.SemaphoreType.DMA
    state = (POLES, BLK)
    return pl.pallas_call(
        functools.partial(comm_kernel, nsb, nch),
        out_shape=(
            *[jax.ShapeDtypeStruct((TOK, width), BF16)] * 3,
            *[jax.ShapeDtypeStruct((POLES, nch * TOK), F32)] * 2,
            jax.ShapeDtypeStruct((1, nch * width), F32),
        ),
        in_specs=[pl.BlockSpec(memory_space=pltpu.HBM)] * 7,
        out_specs=(vmem,) * 6,
        scratch_shapes=[
            *[pltpu.VMEM((TOK, width), BF16)] * 4,
            dma((OWN, 4)),
            pltpu.VMEM((POLES, TOK), F32),
            pltpu.VMEM((POLES, TOK), F32),
            pltpu.VMEM((1, width), F32),
            dma((3,)),
            pltpu.VMEM((TOK, POLES), F32),
            pltpu.VMEM((TOK, POLES), F32),
            pltpu.VMEM((TOK, width), BF16),
            pltpu.VMEM((TOK, width), BF16),
            *[pltpu.VMEM((OWN, BLK, TOK), BF16)] * 4,
            pltpu.VMEM((OWN, GROUP, TOK), F32),
            pltpu.VMEM((OWN, GROUP, TOK), F32),
            pltpu.VMEM((TOK, width), F32),
            pltpu.VMEM((TOK, width), F32),
            *[pltpu.VMEM((OWN, 2) + state, BF16)] * 4,
            pltpu.VMEM((2,) + state, BF16),
            pltpu.VMEM((nsb // 2,) + state, BF16),
            pltpu.VMEM((OWN, 2) + state, BF16),
            pltpu.VMEM((OWN, 2) + state, BF16),
            pltpu.VMEM((OWN, 4, BLK), F32),
            pltpu.VMEM((OWN, 4, BLK), F32),
            pltpu.VMEM((2, 3 * BLK // 2), BF16),
            pltpu.VMEM((nsb // 2, 2, 3 * BLK // 2), BF16),
            pltpu.VMEM((2, 3 * BLK // 2), BF16),
            pltpu.VMEM((2 * nch * OWN, 2, 3 * BLK // 2), BF16),
            pltpu.VMEM((nsb // 2,) + state, F32),
            pltpu.VMEM((OWN * BLK, TOK), BF16),
            pltpu.VMEM((2,) + state, BF16),
            pltpu.VMEM((2,) + state, BF16),
            dma((2,)),
            dma((OWN,)), dma((OWN,)),
            dma((OWN,)), dma((OWN,)),
            dma((nsb // 2,)), dma((nsb // 2,)),
            dma((OWN,)), dma((OWN,)),
            dma((OWN,)), dma((OWN,)),
            dma((nsb // 2,)), dma((nsb // 2,)),
            dma((2 * nch * OWN,)), dma((2 * nch * OWN,)),
        ],
        compiler_params=pltpu.CompilerParams(
            collective_id=0, has_side_effects=True, vmem_limit_bytes=48 << 20
        ),
        name="exchange",
    )(
        *[
            pltpu.with_memory_space_constraint(val, pltpu.HBM)
            for val in (queries, key_input, value_input, cotangent, residues, log_rates, skip_row)
        ]
    )


def store_kernel(*refs):
    count = (len(refs) - 1) // 2
    sem = refs[-1]
    copies = [pltpu.make_async_copy(refs[n], refs[count + n], sem.at[n]) for n in range(count)]
    for copy in copies:
        copy.start()
    for copy in copies:
        copy.wait()


def store(*arrays):
    count = len(arrays)
    return pl.pallas_call(
        store_kernel,
        out_shape=tuple(jax.ShapeDtypeStruct(val.shape, val.dtype) for val in arrays),
        in_specs=[pl.BlockSpec(memory_space=pltpu.VMEM)] * count,
        out_specs=(pl.BlockSpec(memory_space=pltpu.HBM),) * count,
        scratch_shapes=[pltpu.SemaphoreType.DMA((count,))],
        compiler_params=pltpu.CompilerParams(vmem_limit_bytes=1 << 20),
        name="store",
    )(*arrays)


def local(queries, key_input, value_input, cotangent, residues, log_rates, skip_gain):
    gq, gk, gv, gr, gl, gs = store(*exchange(
        queries, key_input, value_input, cotangent, residues.T, log_rates.T, skip_gain.reshape(1, -1)
    ))
    return (gq, gk, gv, gr.T, gl.T, gs.reshape(-1))


def solution(mesh):
    placed = (P("ctx", "ch"), P("ctx", "ch"), P("ctx", "ch"), P("ctx", "ch"), P(), P(), P())
    return jax.shard_map(
        local,
        mesh=mesh,
        in_specs=placed,
        out_specs=(P("ctx", "ch"), P("ctx", "ch"), P("ctx", "ch"), P(), P(), P()),
        check_vma=False,
    )
```

```python
import functools
import math

import jax
import jax.numpy as jnp
from jax import lax
from jax.experimental import pallas as pl
from jax.experimental.pallas import tpu as pltpu
from jax.sharding import PartitionSpec as P

GROUP = 16
POLES = 16
OWN = 8
BLK = 256
TOK = 128

MESH = pl.DeviceIdType.MESH
F32 = jnp.float32
BF16 = jnp.bfloat16
HIGHEST = lax.Precision.HIGHEST


def iota(shape, dim):
    return lax.broadcasted_iota(jnp.int32, shape, dim)


def dot(a, b, dims=((1,), (0,)), precision=None):
    return lax.dot_general(
        a, b, (dims, ((), ())), precision=precision, preferred_element_type=F32
    )


def comm_kernel(
    nsb, nch,
    q_hbm, k_hbm, v_hbm, c_hbm, res_hbm, log_hbm, skip_hbm,
    gq_ref, gk_ref, gv_ref, gr_ref, gl_ref, gs_ref,
    q_ref, k_ref, v_ref, c_ref, in_sem, log_ref, res_ref, skip_ref, par_sem, lam_s, res_s,
    x_s, d_s, ed_s, el_s, ed2_s, el2_s, h_s, hr_s, zl_s, fl_s,
    p1s, p1r, pms, pmr, p2s, p2r, p3s, p3r, pbs, pbr, p4s, p4r, p5s, p5r, coef_s, place_s, swap_s, swap_r, sh,
    s1, r1, sm, rm, s2, r2, s3, r3, sb_, rb_, s4, r4, s5, r5,
):
    ctx = lax.axis_index("ctx")
    ch = lax.axis_index("ch")
    own = ctx % OWN
    sup = ctx // OWN
    col = sup // 2
    half = sup % 2
    ncol = nsb // 2
    plane = 2 * nch * OWN
    here = (half * nch + ch) * OWN + own

    def load(i, n):
        cols = pl.ds(pl.multiple_of(i * BLK, BLK), BLK)
        src, dst = ((q_hbm, q_ref), (k_hbm, k_ref), (v_hbm, v_ref), (c_hbm, c_ref))[n]
        return pltpu.make_async_copy(src.at[:, cols], dst.at[:, cols], in_sem.at[i, n])

    shard = pl.ds(pl.multiple_of(ch * TOK, TOK), TOK)
    wide_shard = pl.ds(pl.multiple_of(ch * (OWN * BLK), OWN * BLK), OWN * BLK)
    params = [
        pltpu.make_async_copy(log_hbm.at[:, shard], log_ref, par_sem.at[0]),
        pltpu.make_async_copy(res_hbm.at[:, shard], res_ref, par_sem.at[1]),
        pltpu.make_async_copy(skip_hbm.at[:, wide_shard], skip_ref, par_sem.at[2]),
    ]
    for copy in params:
        copy.start()

    @pl.loop(0, OWN)
    def _(i):
        for n in range(4):
            load(i, n).start()

    barrier = pltpu.get_barrier_semaphore()

    def greet(ctx_to, ch_to):
        pl.semaphore_signal(barrier, inc=1, device_id=(ctx_to, ch_to), device_id_type=MESH)

    @pl.loop(1, plane)
    def _(n):
        there = (here + n) % plane
        greet((col * 2 + there // (nch * OWN)) * OWN + there % OWN, (there // OWN) % nch)

    @pl.loop(1, ncol)
    def _(j):
        greet((((col + j) % ncol) * 2 + half) * OWN + own, ch)

    lane_t = iota((GROUP, TOK), 1).astype(F32)
    same_group = (iota((BLK, BLK), 0) % 16) == (iota((BLK, BLK), 1) // 16)
    pick_pole = ((iota((POLES, BLK), 1) // 16) == iota((POLES, BLK), 0)).astype(BF16)
    spread_pole = ((iota((BLK, POLES), 0) // 16) == iota((BLK, POLES), 1)).astype(BF16)

    for copy in params:
        copy.wait()
    lam_s[...] = jnp.exp(log_ref[...]).T
    res_s[...] = res_ref[...].T

    @pl.loop(0, OWN)
    def _(i):
        rows = pl.ds(pl.multiple_of(i * 16, 16), 16)
        lam = lam_s[rows, :]
        for p in range(POLES):
            lam_p = lam[:, p : p + 1]
            at = pl.ds(p * 16, 16)
            ed_s[i, at, :] = jnp.exp(-lam_p * lane_t).astype(BF16)
            el_s[i, at, :] = jnp.exp(-lam_p * (TOK - 1.0 - lane_t)).astype(BF16)

    @pl.loop(0, OWN)
    def _(i):
        cols = pl.ds(pl.multiple_of(i * BLK, BLK), BLK)
        for n in range(4):
            load(i, n).wait()
        x = (k_ref[:, cols].astype(F32) * v_ref[:, cols].astype(F32)).astype(BF16)
        d = (c_ref[:, cols].astype(F32) * q_ref[:, cols].astype(F32)).astype(BF16)
        x_s[:, cols] = x
        d_s[:, cols] = d
        for n, (table, val) in enumerate(((el_s, x), (ed_s, d))):
            full = jnp.where(same_group, dot(table[i], val), 0.0).astype(BF16)
            p1s[i, n] = dot(pick_pole, full).astype(BF16)

    pl.semaphore_wait(barrier, (plane - 1) + (ncol - 1))

    def to_own(j, src, dst, send, recv):
        other = (own + j) % OWN
        return pltpu.make_async_remote_copy(
            src_ref=src.at[other], dst_ref=dst.at[own], send_sem=send.at[other], recv_sem=recv.at[own],
            device_id=(sup * OWN + other, ch), device_id_type=MESH,
        )

    def from_own(j, src, dst, send, recv):
        other = (own + j) % OWN
        return pltpu.make_async_remote_copy(
            src_ref=src.at[other], dst_ref=dst.at[other], send_sem=send.at[other], recv_sem=recv.at[other],
            device_id=(sup * OWN + other, ch), device_id_type=MESH,
        )

    def send_own(*args):
        @pl.loop(1, OWN)
        def _(j):
            to_own(j, *args).start()

    def wait_own(*args):
        @pl.loop(1, OWN)
        def _(j):
            from_own(j, *args).wait_recv()

    def sent_own(*args):
        @pl.loop(1, OWN)
        def _(j):
            from_own(j, *args).wait_send()

    send_own(p1s, p1r, s1, r1)
    p1r[own] = p1s[own]

    row_t = iota((TOK, TOK), 0)
    col_t = iota((TOK, TOK), 1)
    lane_group = iota((TOK, BLK), 1) // 16

    lane_row = iota((16, BLK), 1)
    diag = (lane_row % 16) == iota((16, BLK), 0)
    flip = (row_t == TOK - 1 - col_t).astype(BF16)

    @pl.loop(0, OWN)
    def _(i):
        cols = pl.ds(pl.multiple_of(i * BLK, BLK), BLK)
        x = dot(flip, x_s[:, cols]).astype(BF16)
        d = d_s[:, cols]
        pbs[i, 2:3, :] = jnp.sum(x_s[:, cols].astype(F32) * d.astype(F32), axis=0, keepdims=True)
        lam = lam_s[pl.ds(pl.multiple_of(i * 16, 16), 16), :]
        for p in range(POLES):
            ed2_s[i, pl.ds(p * 16, 16), :] = (jnp.exp(-lam[:, p : p + 1] * lane_t) * (lane_t + 1.0)).astype(BF16)
        sums = []
        for g in range(16):
            dm = jnp.where(lane_group == g, d, jnp.zeros_like(d))
            corr = dot(x, dm, ((1,), (1,)))
            corr = jnp.where(col_t >= TOK - 1 - row_t, corr, 0.0)
            corr = pltpu.roll(corr, 1, 1, stride=1, stride_axis=0)
            sums.append(jnp.sum(corr, axis=0, keepdims=True))
        fg = jnp.concatenate(sums, axis=0)
        hi = fg.astype(BF16)
        lo = (fg - hi.astype(F32)).astype(BF16)
        both = jnp.concatenate([hi, lo], axis=0)
        r_in = dot(both, ed_s[i], ((1,), (1,)))
        m_in = dot(both, ed2_s[i], ((1,), (1,)))
        r_in = r_in[:16] + r_in[16:]
        m_in = m_in[:16] + m_in[16:] - r_in
        pbs[i, 0:1, :] = jnp.sum(jnp.where(diag, r_in, 0.0), axis=0, keepdims=True)
        pbs[i, 1:2, :] = jnp.sum(jnp.where(diag, m_in, 0.0), axis=0, keepdims=True)
        pbs[i, 3:4, :] = jnp.zeros((1, BLK), F32)

    send_own(pbs, pbr, sb_, rb_)
    pbr[own] = pbs[own]

    rows = pl.ds(pl.multiple_of(own * 16, 16), 16)
    lam_own = lam_s[rows, :]
    res_own = res_s[rows, :]
    to_chan = ((iota((16, BLK), 1) // 16) == iota((16, BLK), 0)).astype(F32)
    lam_pc = dot(lam_own, to_chan, ((0,), (0,)), HIGHEST)
    res_pc = dot(res_own, to_chan, ((0,), (0,)), HIGHEST)
    w = jnp.exp(-float(TOK) * lam_pc)
    e1 = jnp.exp(-lam_pc)
    re1 = res_pc * e1

    wait_own(p1s, p1r, s1, r1)
    sum_l = jnp.zeros((POLES, BLK), F32)
    sum_d = jnp.zeros((POLES, BLK), F32)
    for b in range(OWN):
        sum_l = w * sum_l + p1r[b, 0].astype(F32)
        sum_d = w * sum_d + p1r[OWN - 1 - b, 1].astype(F32)
    p2s[0] = sum_l.astype(BF16)
    p2s[1] = sum_d.astype(BF16)


    def col_copy(j, slot):
        other = (col + j) % ncol
        later = (other > col).astype(jnp.int32)
        return pltpu.make_async_remote_copy(
            src_ref=p2s.at[1 - later], dst_ref=p2r.at[slot], send_sem=s2.at[other], recv_sem=r2.at[slot],
            device_id=((other * 2 + half) * OWN + own, ch), device_id_type=MESH,
        )

    def half_copy():
        return pltpu.make_async_remote_copy(
            src_ref=swap_s, dst_ref=swap_r, send_sem=sh.at[0], recv_sem=sh.at[1],
            device_id=((col * 2 + 1 - half) * OWN + own, ch), device_id_type=MESH,
        )

    @pl.loop(1, ncol)
    def _(j):
        col_copy(j, col).start()

    scale = dot(
        -lam_own * res_own, ((iota((POLES, BLK), 1) // 16) == iota((POLES, BLK), 0)).astype(F32), precision=HIGHEST
    )
    scale_row = jnp.sum(jnp.where(diag, scale, 0.0), axis=0, keepdims=True)

    @pl.loop(0, ncol)
    def _(b):
        gap = jnp.maximum(jnp.abs(col - b) - 1, 0).astype(F32) * float(TOK * OWN * 2)
        coef_s[b] = jnp.exp(-lam_pc * gap)

    wide_w = jnp.exp(-float(TOK * OWN) * lam_pc)
    wide_w2 = jnp.exp(-float(TOK * OWN * 2) * lam_pc)

    place_s[...] = (
        (iota((OWN * BLK, TOK), 0) // BLK == iota((OWN * BLK, TOK), 1) // 16)
        & (iota((OWN * BLK, TOK), 0) % 16 == iota((OWN * BLK, TOK), 1) % 16)
    ).astype(BF16)
    @pl.loop(0, OWN)
    def _(i):
        rows = pl.ds(pl.multiple_of(i * 16, 16), 16)
        cols = pl.ds(pl.multiple_of(i * BLK, BLK), BLK)
        lam = lam_s[rows, :]
        res = res_s[rows, :]
        taps = jnp.zeros((GROUP, TOK), F32)
        back = jnp.zeros((GROUP, TOK), F32)
        for p in range(POLES):
            lam_p = lam[:, p : p + 1]
            res_p = res[:, p : p + 1]
            ed = jnp.exp(-lam_p * lane_t)
            el = jnp.exp(-lam_p * (TOK - 1.0 - lane_t))
            at = pl.ds(p * 16, 16)
            el2_s[i, at, :] = (el * (TOK - 1.0 - lane_t)).astype(BF16)
            taps = taps + res_p * ed
            back = back + (res_p * jnp.exp(-lam_p)) * el
        h_s[i] = taps
        hr_s[i] = jnp.where(lane_t == 0.0, taps, back)
        x = x_s[:, cols]
        d = d_s[:, cols]
        for n, (table, val) in enumerate(((el2_s, x), (ed2_s, d))):
            full = jnp.where(same_group, dot(table[i], val), 0.0).astype(BF16)
            pms[i, n] = dot(pick_pole, full).astype(BF16)

    send_own(pms, pmr, sm, rm)
    pmr[own] = pms[own]

    zero = jnp.zeros((POLES, BLK), F32)

    def gather(j, sums):
        other = (col + j) % ncol
        col_copy(j, other).wait_recv()
        term = coef_s[other] * p2r[other].astype(F32)
        later = other > col
        return sums[0] + jnp.where(later, 0.0, term), sums[1] + jnp.where(later, term, 0.0)

    col_s, col_f = lax.fori_loop(1, ncol, gather, (zero, zero))
    swap_s[0] = jnp.where(half == 0, sum_l + wide_w2 * col_s, col_s).astype(BF16)
    swap_s[1] = jnp.where(half == 0, col_f, sum_d + wide_w2 * col_f).astype(BF16)
    half_copy().start()

    @pl.loop(0, OWN)
    def _(i):
        cols = pl.ds(pl.multiple_of(i * BLK, BLK), BLK)
        x = x_s[:, cols]
        acc = jnp.zeros((TOK, BLK), F32)
        hr = hr_s[i]
        for g in range(16):
            wide = jnp.broadcast_to(hr[g : g + 1, :], (TOK, TOK))
            mat = pltpu.roll(wide, 0, 1, stride=1, stride_axis=0)
            mat = jnp.where(col_t <= row_t, mat, 0.0).astype(BF16)
            acc = jnp.where(lane_group == g, dot(mat, x), acc)
        zl_s[:, cols] = acc

    wait_own(pms, pmr, sm, rm)
    wait_own(pbs, pbr, sb_, rb_)
    part = pbr[0]
    for b in range(1, OWN):
        part = part + pbr[b]

    half_copy().wait_recv()
    in_s = wide_w * col_s + swap_r[0].astype(F32)
    in_f = wide_w * col_f + swap_r[1].astype(F32)
    carry_s = []
    for b in range(OWN):
        carry_s.append(in_s)
        p3s[b, 0] = (re1 * in_s).astype(BF16)
        in_s = w * in_s + p1r[b, 0].astype(F32)
    r_sum = jnp.zeros((POLES, BLK), F32)
    m_sum = jnp.zeros((POLES, BLK), F32)
    for b in reversed(range(OWN)):
        p3s[b, 1] = (re1 * in_f).astype(BF16)
        d_b = p1r[b, 1].astype(F32)
        r_sum = r_sum + d_b * carry_s[b]
        m_sum = (
            m_sum
            + pmr[b, 1].astype(F32) * carry_s[b]
            + pmr[b, 0].astype(F32) * in_f
            + (float(TOK) * w) * (carry_s[b] * in_f)
        )
        in_f = w * in_f + d_b
    def pack(first, second, third):
        half = BLK // 2
        top = jnp.concatenate([first, second[:, :half]], axis=1)
        low = jnp.concatenate([second[:, half:], third], axis=1)
        return jnp.concatenate([top, low], axis=0).astype(BF16)

    def unpack(val):
        half = BLK // 2
        second = jnp.concatenate([val[0:1, BLK:], val[1:2, :half]], axis=1)
        return val[0:1, :BLK], second, val[1:2, half:]

    chan_group = ((iota((BLK, BLK), 0) // 16) == (iota((BLK, BLK), 1) % 16)).astype(F32)
    pole_row = (iota((POLES, BLK), 1) // 16) == iota((POLES, BLK), 0)
    sums = dot(jnp.concatenate([r_sum * e1, m_sum * e1], axis=0), chan_group, precision=HIGHEST)
    r_row = jnp.sum(jnp.where(pole_row, sums[:POLES], 0.0), axis=0, keepdims=True)
    m_row = jnp.sum(jnp.where(pole_row, sums[POLES:], 0.0), axis=0, keepdims=True)
    p4s[...] = pack(part[0:1] + r_row, part[1:2] + m_row, part[2:3])

    def grad_copy(j, slot):
        other = (col + j) % ncol
        return pltpu.make_async_remote_copy(
            src_ref=p4s, dst_ref=p4r.at[slot], send_sem=s4.at[other], recv_sem=r4.at[slot],
            device_id=((other * 2 + half) * OWN + own, ch), device_id_type=MESH,
        )

    @pl.loop(1, ncol)
    def _(j):
        grad_copy(j, col).start()

    send_own(p3s, p3r, s3, r3)
    p3r[own] = p3s[own]
    p4r[col] = p4s[...]

    length = float(TOK * OWN * nsb)

    @pl.loop(1, ncol)
    def _(j):
        grad_copy(j, (col + j) % ncol).wait_recv()

    total = p4r[0].astype(F32)
    for b in range(1, ncol):
        total = total + p4r[b].astype(F32)
    r_row, m_row, k_row = unpack(total)
    p5s[...] = pack(r_row / length, m_row * scale_row / math.sqrt(length), k_row / math.sqrt(length))

    def last_copy(n, mine):
        there = (here + n) % plane
        slot = here if mine else there
        return pltpu.make_async_remote_copy(
            src_ref=p5s, dst_ref=p5r.at[slot], send_sem=s5.at[there], recv_sem=r5.at[slot],
            device_id=((col * 2 + there // (nch * OWN)) * OWN + there % OWN, (there // OWN) % nch),
            device_id_type=MESH,
        )

    for n in range(1, plane):
        last_copy(n, True).start()
    p5r[here] = p5s[...]

    @pl.loop(0, OWN)
    def _(i):
        cols = pl.ds(pl.multiple_of(i * BLK, BLK), BLK)
        d = d_s[:, cols]
        acc = jnp.zeros((TOK, BLK), F32)
        h = h_s[i]
        for g in range(16):
            wide = jnp.broadcast_to(h[g : g + 1, :], (TOK, TOK))
            mat = pltpu.roll(wide, 0, 1, stride=1, stride_axis=0)
            mat = jnp.where(col_t >= row_t, mat, 0.0).astype(BF16)
            acc = jnp.where(lane_group == g, dot(mat, d), acc)
        fl_s[:, cols] = acc

    @pl.loop(0, OWN)
    def _(j):
        i = (own + j) % OWN

        @pl.when(j > 0)
        def _():
            from_own(j, p3s, p3r, s3, r3).wait_recv()

        cols = pl.ds(pl.multiple_of(i * BLK, BLK), BLK)
        skip = skip_ref[:, cols]
        both = []
        for n, (table, src, loc) in enumerate(((ed_s, x_s, zl_s), (el_s, d_s, fl_s))):
            wide = dot(spread_pole, p3r[i, n])
            wide = jnp.where(same_group, wide, 0.0).astype(BF16)
            corr = dot(table[i], wide, ((0,), (0,)))
            out = skip * src[:, cols].astype(F32) + (loc[:, cols] + corr)
            both.append(out.astype(BF16).astype(F32))
        hidden, flow = both
        gq_ref[:, cols] = (c_ref[:, cols].astype(F32) * hidden).astype(BF16)
        gk_ref[:, cols] = (flow * v_ref[:, cols].astype(F32)).astype(BF16)
        gv_ref[:, cols] = (flow * k_ref[:, cols].astype(F32)).astype(BF16)

    sent_own(p1s, p1r, s1, r1)
    sent_own(pms, pmr, sm, rm)
    sent_own(pbs, pbr, sb_, rb_)
    sent_own(p3s, p3r, s3, r3)

    half_copy().wait_send()

    @pl.loop(1, ncol)
    def _(j):
        col_copy(j, col).wait_send()

    @pl.loop(1, ncol)
    def _(j):
        grad_copy(j, col).wait_send()

    @pl.loop(1, plane)
    def _(n):
        last_copy(n, True).wait_send()

    @pl.loop(1, plane)
    def _(n):
        last_copy(n, False).wait_recv()

    keep = (iota((POLES, OWN * BLK), 1) % BLK) // 16 == iota((POLES, OWN * BLK), 0)
    for i in range(nch):
        rows = [
            unpack(p5r[i * OWN + j].astype(F32) + p5r[(nch + i) * OWN + j].astype(F32)) for j in range(OWN)
        ]
        parts = []
        for n in range(2):
            row = jnp.concatenate([val[n] for val in rows], axis=1)
            parts.append(jnp.where(keep, jnp.broadcast_to(row, keep.shape), 0.0).astype(BF16))
        got = dot(jnp.concatenate(parts, axis=0), place_s[...])
        gr_ref[:, i * TOK : (i + 1) * TOK] = got[:POLES]
        gl_ref[:, i * TOK : (i + 1) * TOK] = got[POLES:]
        for j in range(OWN):
            n = i * OWN + j
            gs_ref[:, n * BLK : (n + 1) * BLK] = rows[j][2]


def exchange(queries, key_input, value_input, cotangent, residues, log_rates, skip_row):
    nsb = lax.axis_size("ctx") // OWN
    nch = lax.axis_size("ch")
    width = OWN * BLK
    vmem = pl.BlockSpec(memory_space=pltpu.VMEM)
    dma = pltpu.SemaphoreType.DMA
    state = (POLES, BLK)
    return pl.pallas_call(
        functools.partial(comm_kernel, nsb, nch),
        out_shape=(
            *[jax.ShapeDtypeStruct((TOK, width), BF16)] * 3,
            *[jax.ShapeDtypeStruct((POLES, nch * TOK), F32)] * 2,
            jax.ShapeDtypeStruct((1, nch * width), F32),
        ),
        in_specs=[pl.BlockSpec(memory_space=pltpu.HBM)] * 7,
        out_specs=(vmem,) * 6,
        scratch_shapes=[
            *[pltpu.VMEM((TOK, width), BF16)] * 4,
            dma((OWN, 4)),
            pltpu.VMEM((POLES, TOK), F32),
            pltpu.VMEM((POLES, TOK), F32),
            pltpu.VMEM((1, width), F32),
            dma((3,)),
            pltpu.VMEM((TOK, POLES), F32),
            pltpu.VMEM((TOK, POLES), F32),
            pltpu.VMEM((TOK, width), BF16),
            pltpu.VMEM((TOK, width), BF16),
            *[pltpu.VMEM((OWN, BLK, TOK), BF16)] * 4,
            pltpu.VMEM((OWN, GROUP, TOK), F32),
            pltpu.VMEM((OWN, GROUP, TOK), F32),
            pltpu.VMEM((TOK, width), F32),
            pltpu.VMEM((TOK, width), F32),
            *[pltpu.VMEM((OWN, 2) + state, BF16)] * 4,
            pltpu.VMEM((2,) + state, BF16),
            pltpu.VMEM((nsb // 2,) + state, BF16),
            pltpu.VMEM((OWN, 2) + state, BF16),
            pltpu.VMEM((OWN, 2) + state, BF16),
            pltpu.VMEM((OWN, 4, BLK), F32),
            pltpu.VMEM((OWN, 4, BLK), F32),
            pltpu.VMEM((2, 3 * BLK // 2), BF16),
            pltpu.VMEM((nsb // 2, 2, 3 * BLK // 2), BF16),
            pltpu.VMEM((2, 3 * BLK // 2), BF16),
            pltpu.VMEM((2 * nch * OWN, 2, 3 * BLK // 2), BF16),
            pltpu.VMEM((nsb // 2,) + state, F32),
            pltpu.VMEM((OWN * BLK, TOK), BF16),
            pltpu.VMEM((2,) + state, BF16),
            pltpu.VMEM((2,) + state, BF16),
            dma((2,)),
            dma((OWN,)), dma((OWN,)),
            dma((OWN,)), dma((OWN,)),
            dma((nsb // 2,)), dma((nsb // 2,)),
            dma((OWN,)), dma((OWN,)),
            dma((OWN,)), dma((OWN,)),
            dma((nsb // 2,)), dma((nsb // 2,)),
            dma((2 * nch * OWN,)), dma((2 * nch * OWN,)),
        ],
        compiler_params=pltpu.CompilerParams(
            collective_id=0, has_side_effects=True, vmem_limit_bytes=48 << 20
        ),
        name="exchange",
    )(
        *[
            pltpu.with_memory_space_constraint(val, pltpu.HBM)
            for val in (queries, key_input, value_input, cotangent, residues, log_rates, skip_row)
        ]
    )


def store_kernel(*refs):
    count = (len(refs) - 1) // 2
    sem = refs[-1]
    copies = [pltpu.make_async_copy(refs[n], refs[count + n], sem.at[n]) for n in range(count)]
    for copy in copies:
        copy.start()
    for copy in copies:
        copy.wait()


def store(*arrays):
    count = len(arrays)
    return pl.pallas_call(
        store_kernel,
        out_shape=tuple(jax.ShapeDtypeStruct(val.shape, val.dtype) for val in arrays),
        in_specs=[pl.BlockSpec(memory_space=pltpu.VMEM)] * count,
        out_specs=(pl.BlockSpec(memory_space=pltpu.HBM),) * count,
        scratch_shapes=[pltpu.SemaphoreType.DMA((count,))],
        compiler_params=pltpu.CompilerParams(vmem_limit_bytes=1 << 20),
        name="store",
    )(*arrays)


def local(queries, key_input, value_input, cotangent, residues, log_rates, skip_gain):
    gq, gk, gv, gr, gl, gs = store(*exchange(
        queries, key_input, value_input, cotangent, residues.T, log_rates.T, skip_gain.reshape(1, -1)
    ))
    return (gq, gk, gv, gr.T, gl.T, gs.reshape(-1))


def solution(mesh):
    placed = (P("ctx", "ch"), P("ctx", "ch"), P("ctx", "ch"), P("ctx", "ch"), P(), P(), P())
    return jax.shard_map(
        local,
        mesh=mesh,
        in_specs=placed,
        out_specs=(P("ctx", "ch"), P("ctx", "ch"), P("ctx", "ch"), P(), P(), P()),
        check_vma=False,
    )
```
